32 devices in a mesh: batch: 8 (over y, x, core), seq: 4 (over z).
Axes of the slice: x: 2, y: 2, z: 4, core: 2. Of those that a mesh axis runs over, the one named last changes fastest.
Arguments:
- tokens: float32 [16, 2048, 768], P('batch', 'seq'), may hold values from -6 to 6
- cotangent: float32 [16, 2048, 768], P('batch', 'seq'), may hold values from -6 to 6
- query_weight: float32 [768, 768], P(('batch', 'seq')), may hold values from -0.4375 to 0.4375
- key_weight: float32 [768, 768], P(('batch', 'seq')), may hold values from -0.21875 to 0.21875
- value_weight: float32 [768, 768], P(('batch', 'seq')), may hold values from -0.21875 to 0.21875
- output_weight: float32 [768, 768], P(('batch', 'seq')), may hold values from -1.25 to 1.25
- up_weight: float32 [768, 3072], P(('batch', 'seq')), may hold values from -0.21875 to 0.21875
- down_weight: float32 [3072, 768], P(('batch', 'seq')), may hold values from -0.109375 to 0.109375
- query_bias: float32 [768], P(('batch', 'seq')), may hold values from -3 to 3
- value_bias: float32 [768], P(('batch', 'seq')), may hold values from -0.6 to 0.6
- output_bias: float32 [768], P(('batch', 'seq')), may hold values from -1.8 to 1.8
- up_bias: float32 [3072], P(('batch', 'seq')), may hold values from -3 to 3
- down_bias: float32 [768], P(('batch', 'seq')), may hold values from -1.8 to 1.8
- first_gain: float32 [768], P(('batch', 'seq')), may hold values from 0.5 to 1.5
- first_shift: float32 [768], P(('batch', 'seq')), may hold values from -1.8 to 1.8
- second_gain: float32 [768], P(('batch', 'seq')), may hold values from 0.5 to 1.5
- second_shift: float32 [768], P(('batch', 'seq')), may hold values from -1.8 to 1.8
- clip_limits: float32 [1], replicated, may hold values from 1.5 to 2.5
Outputs:
- layer_out: float32 [16, 2048, 768], P('batch', 'seq')
- tokens_grad: float32 [16, 2048, 768], P('batch', 'seq')
- query_weight_grad: float32 [768, 768], P(('batch', 'seq'))
- key_weight_grad: float32 [768, 768], P(('batch', 'seq'))
- value_weight_grad: float32 [768, 768], P(('batch', 'seq'))
- output_weight_grad: float32 [768, 768], P(('batch', 'seq'))
- up_weight_grad: float32 [768, 3072], P(('batch', 'seq'))
- down_weight_grad: float32 [3072, 768], P(('batch', 'seq'))
- query_bias_grad: float32 [768], P(('batch', 'seq'))
- value_bias_grad: float32 [768], P(('batch', 'seq'))
- output_bias_grad: float32 [768], P(('batch', 'seq'))
- up_bias_grad: float32 [3072], P(('batch', 'seq'))
- down_bias_grad: float32 [768], P(('batch', 'seq'))
- first_gain_grad: float32 [768], P(('batch', 'seq'))
- first_shift_grad: float32 [768], P(('batch', 'seq'))
- second_gain_grad: float32 [768], P(('batch', 'seq'))
- second_shift_grad: float32 [768], P(('batch', 'seq'))
The draws below stay inside these ranges and needn't reach their ends.
All inputs are finite; a program needn't handle non-finite values.
Results may differ from the reference program's by a relative error of at most 0.017.
The reference program's roundings to bfloat16 on the way count: a program that leaves them out, or rounds other values in their place, can miss the bound.
Values may be sent and summed in bfloat16 or wider, within the bound.
No kernel may reach another device: no remote copies, remote signals or barrier semaphores. Data moves between devices by JAX's collectives and lax.ppermute only.
A program may use at most 256 MiB of HBM per device.

```python
import jax
import jax.numpy as jnp
from jax import lax

D = 768
H = 12
HD = 64
FF = 3072
LEN = 2048
SEQS = 16


def spiked(entries, rng, source, target, shards_of, factor):
    def block_of(position):
        return (jnp.arange(entries.shape[position]) // (entries.shape[position] // shards_of)).reshape((-1,) + (1,) * (entries.ndim - 1 - position))

    near = jax.random.permutation(rng, shards_of)[block_of(target)]
    other_side = (block_of(target) + shards_of // 2) % shards_of
    return jnp.where((block_of(source) == near) | (block_of(source) == other_side), factor * entries, entries)


def levels(key, extent, cuts, low, largest):
    def one(position, blocks):
        draws = jax.random.uniform(jax.random.fold_in(jax.random.fold_in(key, 6), position), (blocks,), jnp.float32, low / len(cuts), largest / len(cuts))
        return jnp.repeat(jnp.exp(draws), extent[position] // blocks).reshape((-1,) + (1,) * (len(extent) - position - 1))

    loudness = one(*cuts[0])
    for cut in cuts[1:]:
        loudness = loudness * one(*cut)
    return loudness


def noise(own_key, dims, deviation, reach, pieces=(), kind=jnp.bfloat16):
    gain = levels(own_key, dims, pieces, -0.22, 0.18) if pieces else 1.0
    array = jax.random.normal(own_key, dims, jnp.float32) * deviation * gain
    return jnp.minimum(jnp.maximum(array, -reach), reach).astype(kind)


def noise_with(stream_key, shape, scale, reach, split, heavy, dtype=jnp.bfloat16):
    drawn = scale * jax.random.normal(stream_key, shape, jnp.float32)
    if split:
        drawn = drawn * levels(stream_key, shape, split, -0.22, 0.18)
    return jnp.clip(spiked(drawn, jax.random.fold_in(stream_key, 3), *heavy), -reach, reach).astype(dtype)


def setup_inputs(seed: int = 0) -> dict:
    key_of = jax.random.split(jax.random.key(seed), 19)
    return {
        "tokens": noise(key_of[0], (SEQS, LEN, D), 1.0, 6.0, ((0, 8), (1, 4)), jnp.float32),
        "cotangent": noise_with(key_of[1], (SEQS, LEN, D), 1.0, 6.0, ((0, 8), (1, 4)), (0, 2, 8, 2.0), jnp.float32),
        "query_weight": noise(key_of[2], (D, D), (D // 4) ** -0.5, 0.4375, ((0, 32),), jnp.float32),
        "key_weight": noise(key_of[3], (D, D), D ** -0.5, 0.21875, ((0, 32),), jnp.float32),
        "value_weight": noise(key_of[4], (D, D), D ** -0.5, 0.21875, ((0, 32),), jnp.float32),
        "output_weight": noise(key_of[5], (D, D), (D // 32) ** -0.5, 1.25, ((0, 32),), jnp.float32),
        "up_weight": noise(key_of[6], (D, FF), D ** -0.5, 0.21875, ((0, 32),), jnp.float32),
        "down_weight": noise(key_of[7], (FF, D), FF ** -0.5, 0.109375, ((0, 32),), jnp.float32),
        "query_bias": noise(key_of[8], (D,), 0.5, 3.0, ((0, 32),), jnp.float32),
        "value_bias": noise(key_of[9], (D,), 0.1, 0.6, ((0, 32),), jnp.float32),
        "output_bias": noise(key_of[10], (D,), 0.3, 1.8, ((0, 32),), jnp.float32),
        "up_bias": noise(key_of[11], (FF,), 0.5, 3.0, ((0, 32),), jnp.float32),
        "down_bias": noise(key_of[12], (D,), 0.3, 1.8, ((0, 32),), jnp.float32),
        "first_gain": jnp.clip(1.0 + 0.1 * jax.random.normal(key_of[13], (D,), jnp.float32), 0.5, 1.5),
        "first_shift": noise(key_of[14], (D,), 0.3, 1.8, ((0, 32),), jnp.float32),
        "second_gain": jnp.clip(1.0 + 0.1 * jax.random.normal(key_of[15], (D,), jnp.float32), 0.5, 1.5),
        "second_shift": noise(key_of[16], (D,), 0.3, 1.8, ((0, 32),), jnp.float32),
        "clip_limits": jnp.clip(jax.random.uniform(key_of[17], (1,), jnp.float32, 1.5, 2.5), 1.5, 2.5),
    }


@jax.custom_vjp
def low(v):
    return lax.optimization_barrier(v.astype(jnp.bfloat16)).astype(jnp.float32)

@jax.custom_vjp
def low_back(v):
    return v

def low_keep(v):
    return (low(v), None)

def low_pass(kept, grad):
    return (grad,)

def back_keep(v):
    return (v, None)

def back_low(kept, grad):
    return (low(grad),)
low.defvjp(low_keep, low_pass)
low_back.defvjp(back_keep, back_low)
EXACT = lax.Precision.HIGHEST
NORM_EPS = 1e-12

def product(left, right):
    return jnp.dot(left, right, precision=EXACT, preferred_element_type=jnp.float32)

def norm_rows(values, scaling, offset):
    center = values - lax.optimization_barrier(jnp.mean(values, axis=-1, keepdims=True))
    spread = lax.optimization_barrier(jnp.mean(center * center, axis=-1, keepdims=True))
    return center * lax.rsqrt(spread + NORM_EPS) * scaling + offset

def gelu_exact(values):
    return 0.5 * values * (1.0 + jax.scipy.special.erf(values * 0.7071067811865476))

def attend(query_rows, key_rows, value_rows):
    key_count = key_rows.shape[0]
    block_rows = min(512, key_count)
    query_heads = query_rows.reshape(key_count // block_rows, block_rows, H, HD)
    key_heads = key_rows.reshape(key_count, H, HD)
    value_heads = value_rows.reshape(key_count, H, HD)
    head_scale = HD ** (-0.5)

    def one_block(query_block):
        scores = low_back(jnp.einsum('qhd,khd->hqk', query_block, key_heads, precision=EXACT) * head_scale)
        highest = lax.optimization_barrier(jnp.max(scores, axis=-1, keepdims=True))
        weights = jnp.exp(scores - highest)
        weights = weights / lax.optimization_barrier(jnp.sum(weights, axis=-1, keepdims=True))
        return jnp.einsum('hqk,khd->qhd', low(weights), value_heads, precision=EXACT)
    context = lax.map(jax.checkpoint(one_block), query_heads)
    return context.reshape(key_count, H * HD)

def block_layer(tokens, params, limits, clip_limits):
    matrices = [low(jnp.clip(params[number], -limits[number], limits[number])) for number in range(6)]
    vectors = [low(params[number]) for number in range(6, 15)]
    query_matrix, key_matrix, value_matrix, output_matrix, up_matrix, down_matrix = matrices
    query_bias, value_bias, output_bias, up_bias, down_bias, first_gain, first_shift, second_gain, second_shift = vectors
    clipped = low(jnp.clip(tokens, -clip_limits[0], clip_limits[0]))
    query_rows = low(low_back(product(clipped, query_matrix) + query_bias))
    key_rows = low(low_back(product(clipped, key_matrix)))
    value_rows = low(low_back(product(clipped, value_matrix) + value_bias))
    context = low(low_back(attend(query_rows, key_rows, value_rows)))
    branch = low_back(product(context, output_matrix) + output_bias)
    hidden = norm_rows(tokens + branch, first_gain, first_shift)
    hidden_low = low(hidden)
    upward = low_back(product(hidden_low, up_matrix) + up_bias)
    activated = low(gelu_exact(upward))
    downward = low_back(product(activated, down_matrix) + down_bias)
    return norm_rows(hidden + downward, second_gain, second_shift)

def reference(tokens, cotangent, query_weight, key_weight, value_weight, output_weight, up_weight, down_weight, query_bias, value_bias, output_bias, up_bias, down_bias, first_gain, first_shift, second_gain, second_shift, clip_limits):
    params = (query_weight, key_weight, value_weight, output_weight, up_weight, down_weight, query_bias, value_bias, output_bias, up_bias, down_bias, first_gain, first_shift, second_gain, second_shift)
    limits = [0.5 * jnp.max(jnp.abs(params[number])) for number in range(6)]

    def one_sequence(totals, seq_items):
        sequence, seq_cot = seq_items
        result, pullback = jax.vjp(lambda inputs, weights: block_layer(inputs, weights, limits, clip_limits), sequence, params)
        grad_inputs, grad_params = pullback(seq_cot)
        return (tuple((running + update for running, update in zip(totals, grad_params))), (result, grad_inputs))
    zero_grads = tuple((jnp.zeros_like(member) for member in params))
    totals, (layer_out, tokens_grad) = lax.scan(one_sequence, zero_grads, (tokens, cotangent))
    grad_query_matrix, grad_key_matrix, grad_value_matrix, grad_output_matrix, grad_up_matrix, grad_down_matrix, grad_query_bias, grad_value_bias, grad_output_bias, grad_up_bias, grad_down_bias, grad_first_gain, grad_first_shift, grad_second_gain, grad_second_shift = totals
    return (layer_out, tokens_grad, grad_query_matrix, grad_key_matrix, grad_value_matrix, grad_output_matrix, grad_up_matrix, grad_down_matrix, grad_query_bias, grad_value_bias, grad_output_bias, grad_up_bias, grad_down_bias, grad_first_gain, grad_first_shift, grad_second_gain, grad_second_shift)
```

```python
import jax
import jax.numpy as jnp
from jax import lax
from jax.experimental import pallas as pl
from jax.experimental.pallas import tpu as pltpu
from jax.sharding import Mesh, PartitionSpec as P

HD = 64
LANES = 128
NORM_EPS = 1e-12
AXES = ("pair", "core", "seq")
GROUP_PAIRS = 2
SHORT = pl.CostEstimate(flops=1 << 20, transcendentals=0, bytes_accessed=1 << 16)
F32 = jnp.float32
BF16 = jnp.bfloat16

NT = (((1,), (1,)), ((), ()))
NN = (((1,), (0,)), ((), ()))
TN = (((0,), (0,)), ((), ()))


def dots(left, right, dims):
    return lax.dot_general(left, right, dims, preferred_element_type=F32)


def rounded(values):
    return lax.reduce_precision(values, 8, 7)


def project(here, limit, tokens, pieces, biases):
    rows, width = tokens[0].shape
    pairs = len(pieces) // 2
    piece_rows, columns = pieces[0].shape
    block = min(256, rows)
    steps = rows // block

    def kernel(here_ref, limit_ref, own_ref, other_ref, bias_ref, *refs):
        pieces_refs, (q_ref, kv_ref, matrix_ref, held, sems) = refs[: 2 * pairs], refs[2 * pairs :]
        step = pl.program_id(0)
        pair, core = here_ref[0], here_ref[1]
        matrix = held.reshape(2 * pairs * piece_rows, columns)
        store = pltpu.make_async_copy(matrix, matrix_ref, sems.at[2 * pairs])

        @pl.when(step == 0)
        def _():
            loads = []
            for number, piece in enumerate(pieces_refs):
                place = pair ^ (number // 2)
                half = core if number % 2 == 0 else 1 - core
                loads.append(pltpu.make_async_copy(piece, held.at[place, half], sems.at[number]))
            for copy in loads:
                copy.start()
            for copy in loads:
                copy.wait()
            slots = [(place, half) for place in range(pairs) for half in range(2)]
            for number in range(3):
                lanes = slice(width * number, width * (number + 1))
                largest = jnp.zeros((piece_rows, width), F32)
                for place, half in slots:
                    largest = jnp.maximum(largest, jnp.abs(held[place, half, :, lanes].astype(F32)))
                top = jnp.full((1, width), 0.5 * jnp.max(largest), F32).astype(BF16)
                for place, half in slots:
                    held[place, half, :, lanes] = jnp.maximum(jnp.minimum(held[place, half, :, lanes], top), -top)
            store.start()

        top = jnp.full((1, width), limit_ref[0], F32).astype(BF16)

        def clipped(ref):
            return jnp.maximum(jnp.minimum(ref[...], top), -top)

        @pl.when(step < steps)
        def _():
            all_three = dots(clipped(own_ref), matrix[...], NN) + bias_ref[...]
            q_ref[...] = all_three[:, :width].astype(BF16) * jnp.asarray(HD**-0.5, BF16)
            kv_ref[...] = all_three[:, width:].astype(BF16)

        @pl.when(step >= steps)
        def _():
            kv_ref[...] = (dots(clipped(other_ref), matrix[:, width:], NN) + bias_ref[:, width:]).astype(BF16)

        @pl.when(step == 2 * steps - 1)
        def _():
            store.wait()

    any_spec = pl.BlockSpec(memory_space=pl.ANY)
    smem_spec = pl.BlockSpec(memory_space=pltpu.SMEM)
    return pl.pallas_call(
        kernel,
        grid=(2 * steps,),
        in_specs=[
            smem_spec,
            smem_spec,
            pl.BlockSpec((block, width), lambda i: (jnp.minimum(i, steps - 1), 0)),
            pl.BlockSpec((block, width), lambda i: (jnp.maximum(i - steps, 0), 0)),
            pl.BlockSpec((1, columns), lambda i: (0, 0)),
        ]
        + [any_spec] * (2 * pairs),
        out_specs=[
            pl.BlockSpec((block, width), lambda i: (jnp.minimum(i, steps - 1), 0)),
            pl.BlockSpec((block, 2 * width), lambda i: (i, 0)),
            any_spec,
        ],
        out_shape=[
            jax.ShapeDtypeStruct((rows, width), BF16),
            jax.ShapeDtypeStruct((2 * rows, 2 * width), BF16),
            jax.ShapeDtypeStruct((2 * pairs * piece_rows, columns), BF16),
        ],
        scratch_shapes=[
            pltpu.VMEM((pairs, 2, piece_rows, columns), BF16),
            pltpu.SemaphoreType.DMA((2 * pairs + 1,)),
        ],
        compiler_params=pltpu.CompilerParams(vmem_limit_bytes=56 << 20),
        cost_estimate=SHORT,
    )(here, limit, tokens[0], tokens[1], biases, *pieces)


def attend(queries, keys_values, start, count):
    seqs, rows, width = queries.shape
    keys = keys_values.shape[1]
    pairs = width // LANES
    block = min(256, rows)

    def kernel(q_ref, k_ref, v_ref, o_ref, l_ref, p_ref):
        low = lax.broadcasted_iota(jnp.int32, (1, LANES), 1) < HD
        q = q_ref[0]
        outs, inverses = [], []
        for half in range(2):
            mine = low if half == 0 else ~low
            scores = dots(jnp.where(mine, q, jnp.zeros_like(q)), k_ref[0], NT)
            weights = jnp.exp(scores - jnp.max(scores, axis=-1, keepdims=True))
            inverse = 1.0 / jnp.sum(weights, axis=-1, keepdims=True)
            weights = weights.astype(BF16)
            p_ref[0, half] = weights
            outs.append(dots(weights, v_ref[0], NN) * inverse)
            inverses.append(inverse)
        o_ref[0] = jnp.where(low, outs[0], outs[1]).astype(BF16)
        l_ref[0] = jnp.where(low, inverses[0], inverses[1])

    rows_spec = pl.BlockSpec((1, block, LANES), lambda s, p, i: (s, i, p))
    return pl.pallas_call(
        kernel,
        grid=(seqs, count, rows // block),
        in_specs=[
            pl.BlockSpec((1, block, LANES), lambda s, p, i: (s, i, start + p)),
            pl.BlockSpec((1, keys, LANES), lambda s, p, i: (s, 0, start + p)),
            pl.BlockSpec((1, keys, LANES), lambda s, p, i: (s, 0, pairs + start + p)),
        ],
        out_specs=[
            rows_spec,
            rows_spec,
            pl.BlockSpec((1, 2, block, keys), lambda s, p, i: (s, p, i, 0)),
        ],
        out_shape=[
            jax.ShapeDtypeStruct((seqs, rows, count * LANES), BF16),
            jax.ShapeDtypeStruct((seqs, rows, count * LANES), F32),
            jax.ShapeDtypeStruct((seqs, 2 * count, rows, keys), BF16),
        ],
        compiler_params=pltpu.CompilerParams(vmem_limit_bytes=56 << 20),
        cost_estimate=SHORT,
    )(queries, keys_values, keys_values)


def attend_back(queries, keys_values, context, context_grad, weights, start):
    seqs, rows, width = queries.shape
    keys = keys_values.shape[1]
    pairs = width // LANES
    count = context.shape[2] // LANES
    block = min(512, rows)

    def kernel(q_ref, k_ref, v_ref, o_ref, do_ref, p_ref, dq_ref, dk_ref, dv_ref, sums_ref, dk_sum, dv_sum):
        step = pl.program_id(2)
        low = lax.broadcasted_iota(jnp.int32, (1, LANES), 1) < HD
        q, do = q_ref[0], do_ref[0]
        product = do.astype(F32) * o_ref[0].astype(F32)
        q_turned, do_turned = q.T, do.T

        @pl.when(step == 0)
        def _():
            dk_sum[...] = jnp.zeros_like(dk_sum)
            dv_sum[...] = jnp.zeros_like(dv_sum)
            sums_ref[...] = jnp.zeros_like(sums_ref)

        grads = []
        for half in range(2):
            mine = low if half == 0 else ~low
            lanes = slice(half * HD, (half + 1) * HD)
            delta = jnp.sum(jnp.where(mine, product, 0.0), axis=-1, keepdims=True)
            raised = dots(jnp.where(mine, do, jnp.zeros_like(do)), v_ref[0], NT)
            p = p_ref[0, half]
            ds = (raised - delta).astype(BF16) * p
            grads.append(dots(ds, k_ref[0], NN))
            dk_sum[lanes] += dots(q_turned[lanes], ds, NN)
            dv_sum[lanes] += dots(do_turned[lanes], p, NN)
        dq = (jnp.where(low, grads[0], grads[1]) * HD**-0.5).astype(BF16)
        dq_ref[0] = dq
        sums_ref[0, 0:1] += jnp.sum(dq.astype(F32), axis=0, keepdims=True)

        @pl.when(step == pl.num_programs(2) - 1)
        def _():
            dk_ref[0] = dk_sum[...].T.astype(BF16)
            dv = dv_sum[...].T.astype(BF16)
            dv_ref[0] = dv
            sums_ref[0, 1:2] = jnp.sum(dv.astype(F32), axis=0, keepdims=True)

    rows_spec = pl.BlockSpec((1, block, LANES), lambda s, p, i: (s, i, p))
    chosen_spec = pl.BlockSpec((1, block, LANES), lambda s, p, i: (s, i, start + p))
    keys_spec = pl.BlockSpec((1, keys, LANES), lambda s, p, i: (s, 0, p))
    return pl.pallas_call(
        kernel,
        grid=(seqs, count, rows // block),
        in_specs=[
            chosen_spec,
            pl.BlockSpec((1, keys, LANES), lambda s, p, i: (s, 0, start + p)),
            pl.BlockSpec((1, keys, LANES), lambda s, p, i: (s, 0, pairs + start + p)),
            rows_spec,
            chosen_spec,
            pl.BlockSpec((1, 2, block, keys), lambda s, p, i: (s, p, i, 0)),
        ],
        out_specs=[rows_spec, keys_spec, keys_spec, pl.BlockSpec((1, 8, LANES), lambda s, p, i: (s, 0, p))],
        out_shape=[
            jax.ShapeDtypeStruct((seqs, rows, count * LANES), BF16),
            jax.ShapeDtypeStruct((seqs, keys, count * LANES), BF16),
            jax.ShapeDtypeStruct((seqs, keys, count * LANES), BF16),
            jax.ShapeDtypeStruct((seqs, 8, count * LANES), F32),
        ],
        scratch_shapes=[pltpu.VMEM((LANES, keys), F32), pltpu.VMEM((LANES, keys), F32)],
        compiler_params=pltpu.CompilerParams(vmem_limit_bytes=56 << 20),
        cost_estimate=SHORT,
    )(queries, keys_values, keys_values, context, context_grad, weights)


def back_to_tokens(terms, matrix, first_row, rows, finish=None):
    width, columns = matrix.shape
    block = min(256, rows)
    shift = first_row // block
    extra = [] if finish is None else list(finish)

    def kernel(*refs):
        matrix_ref, parts, refs = refs[0], refs[1 : 1 + len(terms)], refs[1 + len(terms) :]
        total = None
        for ref, (part, column) in zip(parts, terms):
            product = dots(ref[...], matrix_ref[:, column : column + part.shape[1]], NT)
            total = product if total is None else total + product
        if finish is not None:
            limit_ref, arrived_ref, zero_ref, tokens_ref, out_ref = refs
            total = total + arrived_ref[...].astype(F32)
            inside = jnp.abs(tokens_ref[...].astype(F32)) < limit_ref[0]
            total = zero_ref[...] + jnp.where(inside, total, 0.0)
        else:
            (out_ref,) = refs
        out_ref[...] = total.astype(BF16)

    row_spec = pl.BlockSpec((block, width), lambda i: (i, 0))
    return pl.pallas_call(
        kernel,
        grid=(rows // block,),
        in_specs=[pl.BlockSpec((width, columns), lambda i: (0, 0), pipeline_mode=pl.Buffered(1))]
        + [pl.BlockSpec((block, part.shape[1]), lambda i: (shift + i, 0)) for part, _ in terms]
        + ([] if finish is None else [pl.BlockSpec(memory_space=pltpu.SMEM)] + [row_spec] * 3),
        out_specs=row_spec,
        out_shape=jax.ShapeDtypeStruct((rows, width), BF16),
        compiler_params=pltpu.CompilerParams(vmem_limit_bytes=56 << 20),
        cost_estimate=SHORT,
    )(matrix, *[part for part, _ in terms], *extra)


def weight_grads(here, limit, tokens, chunks, pairs):
    rows, width = tokens[0].shape
    block = min(256, rows)
    steps = rows // block
    span = chunks[0][0].shape[1]
    piece_rows = width // (2 * pairs)

    def kernel(here_ref, limit_ref, own_ref, other_ref, *refs):
        grads, (mine_ref, theirs_ref, total, held, sems) = refs[: 3 * len(chunks)], refs[3 * len(chunks) :]
        step = pl.program_id(0)
        pair, core = here_ref[0], here_ref[1]
        top = jnp.full((1, width), limit_ref[0], F32).astype(BF16)

        @pl.when(step == 0)
        def _():
            total[...] = jnp.zeros_like(total)

        def add(tokens_ref, kinds):
            turned = jnp.maximum(jnp.minimum(tokens_ref[...], top), -top).T
            for number in range(len(chunks)):
                for kind in kinds:
                    start = width * kind + span * number
                    total[:, start : start + span] += dots(turned, grads[3 * number + kind][...], NN)

        @pl.when(step < steps)
        def _():
            add(own_ref, (0, 1, 2))

        @pl.when(step >= steps)
        def _():
            add(other_ref, (1, 2))

        @pl.when(step == 2 * steps - 1)
        def _():
            held[...] = total[...].astype(BF16).reshape(held.shape)
            stores = []
            for number in range(2 * pairs):
                target = theirs_ref if number % 2 else mine_ref
                place = held.at[pair ^ (number // 2), 1 - core if number % 2 else core]
                stores.append(pltpu.make_async_copy(place, target.at[number // 2], sems.at[number]))
            for copy in stores:
                copy.start()
            for copy in stores:
                copy.wait()

    smem_spec = pl.BlockSpec(memory_space=pltpu.SMEM)
    own_spec = pl.BlockSpec((block, span), lambda i: (jnp.minimum(i, steps - 1), 0))
    all_spec = pl.BlockSpec((block, span), lambda i: (i, 0))
    part = jax.ShapeDtypeStruct((pairs, piece_rows, 3 * width), BF16)
    return pl.pallas_call(
        kernel,
        grid=(2 * steps,),
        in_specs=[
            smem_spec,
            smem_spec,
            pl.BlockSpec((block, width), lambda i: (jnp.minimum(i, steps - 1), 0)),
            pl.BlockSpec((block, width), lambda i: (jnp.maximum(i - steps, 0), 0)),
        ]
        + [own_spec, all_spec, all_spec] * len(chunks),
        out_specs=[pl.BlockSpec(memory_space=pl.ANY)] * 2,
        out_shape=[part, part],
        scratch_shapes=[
            pltpu.VMEM((width, 3 * width), F32),
            pltpu.VMEM((pairs, 2, piece_rows, 3 * width), BF16),
            pltpu.SemaphoreType.DMA((2 * pairs,)),
        ],
        compiler_params=pltpu.CompilerParams(vmem_limit_bytes=56 << 20),
        cost_estimate=SHORT,
    )(here, limit, tokens[0], tokens[1], *[grad for chunk in chunks for grad in chunk])


def middle(here, contexts, inverses, residual, cotangent, weights, vectors, up_bias, shape):
    rows, width = residual.shape
    units = up_bias.shape[1]
    pairs, along = shape
    block = min(256, rows)
    blocks = units // width
    parts = len(weights)
    whole = parts == 2
    groups = len(contexts)
    share = width // (2 * pairs * along)
    if whole:
        first_shape = (pairs, 2, along * share, width + units)
        second_shape = (pairs, 2, along * share * blocks, width)
    else:
        first_shape = (pairs, 2, along, share, width + units)
        second_shape = (pairs, 2, along, blocks, share, width)
    copies = 2 if whole else 2 * pairs * (1 + blocks)

    def kernel(here_ref, residual_ref, cot_ref, vector_ref, bias_ref, *refs):
        context_refs, inverse_refs, refs = refs[:groups], refs[groups : 2 * groups], refs[2 * groups :]
        weight_refs, refs = refs[:parts], refs[parts:]
        result_ref, zero_ref, back_ref, small_ref, small_up_ref, *outs, first, second, grad_output, grad_up, grad_down = refs[:-3]
        act_ref, slope_ref, sems = refs[-3:]
        step = pl.program_id(0)
        pair, core = here_ref[0], here_ref[1]

        def matches(pieces):
            if whole:
                return [(pieces[0], first), (pieces[1], second)]
            found = []
            for number, piece in enumerate(pieces):
                at = pair ^ (number // 2), 1 - core if number % 2 else core
                found.append((piece.at[:, :, : width + units], first.at[at]))
                for j in range(blocks):
                    lanes = slice(width + units + width * j, width + units + width * (j + 1))
                    found.append((piece.at[:, :, lanes], second.at[at].at[:, j]))
            return found

        loads = [
            pltpu.make_async_copy(outside, place, sems.at[i]) for i, (outside, place) in enumerate(matches(weight_refs))
        ]

        @pl.when(step == 0)
        def _():
            for copy in loads:
                copy.start()
            small_ref[...] = jnp.zeros_like(small_ref)
            small_up_ref[...] = jnp.zeros_like(small_up_ref)
            grad_output[...] = jnp.zeros_like(grad_output)
            grad_up[...] = jnp.zeros_like(grad_up)
            grad_down[...] = jnp.zeros_like(grad_down)
            for copy in loads:
                copy.wait()

        def vector(number):
            return vector_ref[number : number + 1]

        def mean(values):
            return jnp.mean(values, axis=-1, keepdims=True)

        def columns(j):
            return slice(width * j, width * (j + 1))

        def output_matrix():
            return first[(..., slice(0, width))].reshape(width, width)

        def up_matrix(j):
            return first[(..., slice(width * (j + 1), width * (j + 2)))].reshape(width, width)

        down_rows = second.reshape(units, width)

        bias_output, bias_down, gain_one, shift_one, gain_two, shift_two = [vector(i) for i in range(6)]
        ctx = jnp.concatenate([ref[...] for ref in context_refs], axis=1)
        zero = residual_ref[...].astype(F32) + dots(ctx, output_matrix(), NN) + bias_output
        center = zero - mean(zero)
        scale_one = lax.rsqrt(mean(center * center) + NORM_EPS)
        normal_one = center * scale_one
        hidden = normal_one * gain_one + shift_one
        hidden_low = hidden.astype(BF16)
        summed = hidden + bias_down
        for j in range(blocks):
            up = dots(hidden_low, up_matrix(j), NN) + bias_ref[:, columns(j)]
            share = 0.5 + 0.5 * lax.erf(up * 0.7071067811865476)
            act = (up * share).astype(BF16)
            act_ref[:, columns(j)] = act
            slope_ref[:, columns(j)] = share + up * (0.3989422804014327 * jnp.exp(-0.5 * up * up))
            summed = summed + dots(act, down_rows[columns(j)], NN)
        center = summed - mean(summed)
        scale_two = lax.rsqrt(mean(center * center) + NORM_EPS)
        normal_two = center * scale_two
        result_ref[...] = (normal_two * gain_two + shift_two).astype(result_ref.dtype)

        cot = cot_ref[...].astype(F32)
        scaled = cot * gain_two
        grad_summed = scale_two * (scaled - mean(scaled) - normal_two * mean(scaled * normal_two))
        down_low = grad_summed.astype(BF16)
        grad_hidden = grad_summed
        for j in range(blocks):
            lifted = dots(down_low, down_rows[columns(j)], NT) * slope_ref[:, columns(j)]
            up_low = lifted.astype(BF16)
            small_up_ref[:, columns(j)] += jnp.sum(up_low.astype(F32), axis=0, keepdims=True)
            grad_up[:, columns(j)] += dots(hidden_low, up_low, TN)
            grad_hidden = grad_hidden + dots(up_low, up_matrix(j), NT)
            grad_down[columns(j)] += dots(act_ref[:, columns(j)], down_low, TN)
        scaled = grad_hidden * gain_one
        grad_zero = scale_one * (scaled - mean(scaled) - normal_one * mean(scaled * normal_one))
        zero_ref[...] = grad_zero
        branch_low = grad_zero.astype(BF16)
        grad_output[...] += dots(ctx, branch_low, TN)
        back_ref[...] = (dots(branch_low, output_matrix(), NT) * jnp.concatenate([ref[...] for ref in inverse_refs], axis=1)).astype(BF16)
        sums = [branch_low.astype(F32), down_low.astype(F32), grad_hidden * normal_one, grad_hidden, cot * normal_two, cot]
        for number, terms in enumerate(sums):
            small_ref[number : number + 1] += jnp.sum(terms, axis=0, keepdims=True)

        @pl.when(step == pl.num_programs(0) - 1)
        def _():
            part = first.shape[:-1] + (width,)
            first[(..., slice(0, width))] = grad_output[...].astype(BF16).reshape(part)
            for j in range(blocks):
                lanes = slice(width * (j + 1), width * (j + 2))
                first[(..., lanes)] = grad_up[:, columns(j)].astype(BF16).reshape(part)
            second[...] = grad_down[...].astype(BF16).reshape(second.shape)
            targets = outs if whole else [outs[i % 2].at[i // 2] for i in range(2 * pairs)]
            stores = [
                pltpu.make_async_copy(place, outside, sems.at[i]) for i, (outside, place) in enumerate(matches(targets))
            ]
            for copy in stores:
                copy.start()
            for copy in stores:
                copy.wait()

    any_spec = pl.BlockSpec(memory_space=pl.ANY)
    row_spec = pl.BlockSpec((block, width), lambda i: (i, 0))
    if whole:
        grads = [jax.ShapeDtypeStruct(first_shape, BF16), jax.ShapeDtypeStruct(second_shape, BF16)]
    else:
        grads = [jax.ShapeDtypeStruct((pairs, along, share, width + 2 * units), BF16)] * 2
    return pl.pallas_call(
        kernel,
        grid=(rows // block,),
        in_specs=[pl.BlockSpec(memory_space=pltpu.SMEM)]
        + [row_spec] * 2
        + [pl.BlockSpec((8, width), lambda i: (0, 0)), pl.BlockSpec((1, units), lambda i: (0, 0))]
        + [pl.BlockSpec((block, part.shape[1]), lambda i: (i, 0)) for part in (*contexts, *inverses)]
        + [any_spec] * parts,
        out_specs=[row_spec] * 3
        + [pl.BlockSpec((8, width), lambda i: (0, 0)), pl.BlockSpec((1, units), lambda i: (0, 0))]
        + [any_spec] * 2,
        out_shape=[
            jax.ShapeDtypeStruct((rows, width), BF16),
            jax.ShapeDtypeStruct((rows, width), F32),
            jax.ShapeDtypeStruct((rows, width), BF16),
            jax.ShapeDtypeStruct((8, width), F32),
            jax.ShapeDtypeStruct((1, units), F32),
            *grads,
        ],
        scratch_shapes=[
            pltpu.VMEM(first_shape, BF16),
            pltpu.VMEM(second_shape, BF16),
            pltpu.VMEM((width, width), F32),
            pltpu.VMEM((width, units), F32),
            pltpu.VMEM((units, width), F32),
            pltpu.VMEM((block, units), BF16),
            pltpu.VMEM((block, units), F32),
            pltpu.SemaphoreType.DMA((copies,)),
        ],
        compiler_params=pltpu.CompilerParams(vmem_limit_bytes=60 << 20),
        cost_estimate=SHORT,
    )(here, residual, cotangent, vectors, up_bias, *contexts, *inverses, *weights)


def after(values, *earlier):
    return lax.optimization_barrier((values, earlier))[0]


class Plan:
    def __init__(self, pairs, along, seqs):
        self.pairs, self.along, self.seqs = pairs, along, seqs
        self.devices = 2 * pairs * along
        self.by_chip = 2 * seqs == along and pairs == 4 and along & (along - 1) == 0

    def moves(self, number):
        table = []
        for pair in range(self.pairs):
            for core in range(2):
                for place in range(self.along):
                    source = (pair * 2 + core) * self.along + place
                    chip = core * self.seqs + (place + number) % self.seqs
                    target = (pair * 2 + place // self.seqs) * self.along + chip
                    table.append((source, target))
        return table

    def choose(self, pieces):
        place = lax.axis_index("seq")
        return [
            lax.dynamic_index_in_dim(pieces, (place + number) % self.seqs, 0, keepdims=False)
            for number in range(self.seqs)
        ]

    def send(self, chosen):
        arrived = [lax.ppermute(part, AXES, self.moves(number)) for number, part in enumerate(chosen)]
        return jnp.concatenate(arrived, axis=0)

    def to_home(self, worked):
        blocks = worked.reshape(self.seqs, -1, worked.shape[-1])
        if not self.by_chip:
            return blocks
        place = lax.axis_index("seq")
        back = [
            lax.ppermute(blocks[number], AXES, [(b, a) for a, b in self.moves(number)]) for number in range(self.seqs)
        ]
        if self.seqs == 2:
            even = place % 2 == 0
            return jnp.stack([jnp.where(even, back[0], back[1]), jnp.where(even, back[1], back[0])])
        order = (jnp.arange(self.seqs) - place) % self.seqs
        return jnp.stack(back)[order]

    def swap(self, values):
        return lax.ppermute(values, "core", [(0, 1), (1, 0)])

    def meet(self, values, axis, far):
        count = lax.axis_size(axis)
        return lax.ppermute(values, axis, [(i, i ^ far) for i in range(count)])

    def column(self, rows):
        here = lax.axis_index("seq")
        held = jnp.zeros((self.along,) + rows.shape, rows.dtype)
        for far in range(self.along):
            piece = self.meet(rows, "seq", far) if far else rows
            held = lax.dynamic_update_index_in_dim(held, piece, here ^ far, 0)
        return held

    def both_cores(self, pieces):
        return [part for piece in pieces for part in (piece, self.swap(piece))]

    def add_cores(self, mine, theirs, *earlier):
        return (mine.astype(F32) + after(self.swap(theirs), *earlier).astype(F32)).astype(BF16)

    def near_and_far(self, column):
        return [column] + [self.meet(column, "pair", far) for far in range(1, self.pairs)]

    def total_along(self, values):
        column = values.reshape(self.along, -1, values.shape[-1])
        here = lax.axis_index("seq")

        def block(far):
            return lax.dynamic_index_in_dim(column, here ^ far, 0, keepdims=False)

        total = block(0).astype(F32)
        for far in range(1, self.along):
            total = total + self.meet(block(far), "seq", far).astype(F32)
        return total

    def total_pairs(self, low):
        total = low[0].astype(F32)
        for far in range(1, self.pairs):
            total = total + self.meet(low[far], "pair", far).astype(F32)
        return total.astype(BF16)

    def gather(self, rows):
        return lax.all_gather(rows, AXES, axis=0, tiled=True)

    def scatter(self, total):
        return lax.psum_scatter(total, AXES, scatter_dimension=0, tiled=True)


def same_side(tokens, limit):
    near = rounded(limit)
    below = jnp.where(near < limit, near, rounded(near * (1.0 - 2.0**-8)))
    above = jnp.where(near < limit, rounded(near * (1.0 + 1.5 * 2.0**-8)), near)
    size = jnp.abs(tokens)
    coarse = rounded(size)
    coarse = jnp.where(size < limit, jnp.minimum(coarse, below), jnp.maximum(coarse, above))
    return jnp.where(tokens < 0, -coarse, coarse).astype(BF16)


def split_three(values):
    high = rounded(values)
    middle_term = rounded(values - high)
    return jnp.concatenate([high, middle_term, values - high - middle_term]).astype(BF16)


def local(plan, tokens, cotangent, *rest):
    params, clip_limits = rest[:15], rest[15]
    limit = clip_limits[0]
    matrices = params[:6]
    width = tokens.shape[-1]
    units = matrices[4].shape[1]
    devices = plan.devices
    here = jnp.stack([lax.axis_index("pair"), lax.axis_index("core")]).astype(jnp.int32)

    if plan.by_chip:
        chosen = plan.choose(same_side(tokens, limit))
        params = after(params, chosen)
        matrices = params[:6]
        coarse = plan.send(chosen)
    else:
        coarse = same_side(tokens, limit).reshape(-1, width)
    largest = jnp.stack([jnp.max(jnp.abs(matrix)) for matrix in matrices])
    packed = jnp.concatenate([vector.astype(BF16) for vector in params[6:]] + [split_three(largest)])
    packed = jnp.pad(packed, (0, -packed.shape[0] % LANES))
    vectors = lax.all_to_all(
        jnp.broadcast_to(packed[None], (devices,) + packed.shape), AXES, split_axis=0, concat_axis=0, tiled=True
    )
    qkv_rows = jnp.concatenate([matrix.astype(BF16) for matrix in matrices[:3]], axis=1)

    vectors = vectors.astype(F32)
    counts = [vector.shape[0] for vector in params[6:]]
    starts = [sum(counts[:i]) for i in range(len(counts) + 1)]
    bias_query, bias_value, bias_output, bias_up, bias_down, gain_one, shift_one, gain_two, shift_two = [
        vectors[:, start : start + count].reshape(-1) for start, count in zip(starts, counts)
    ]
    terms = vectors[:, starts[-1] : starts[-1] + 18]
    limits = 0.5 * jnp.max(terms[:, :6] + terms[:, 6:12] + terms[:, 12:18], axis=0)
    biases = jnp.concatenate([bias_query, jnp.zeros_like(bias_value), bias_value])[None]
    limit_low = limit.astype(BF16)

    def clip_to(number):
        return jnp.clip(matrices[number], -limits[number], limits[number]).astype(BF16)

    first_rows, second_rows = jnp.concatenate([clip_to(3), clip_to(4)], axis=1), clip_to(5)
    if plan.by_chip:
        seqs, keys = 1, 2 * coarse.shape[0]
        qkv_column = plan.column(qkv_rows).reshape(-1, 3 * width)
        qkv_pieces = plan.near_and_far(qkv_column)
        other = plan.swap(after(coarse, vectors))
        rest_rows = [first_rows] + jnp.split(second_rows, units // width, axis=0)
        rest_column = plan.column(after(jnp.concatenate(rest_rows, axis=1), coarse))
        qkv_pieces = plan.both_cores(after(qkv_pieces, rest_column))
        rest_pieces = plan.near_and_far(rest_column)
        cotangent_low = plan.send(after(plan.choose(cotangent.astype(BF16)), rest_column))
        queries, keys_values, matrix = project(here, clip_limits, [coarse, other], qkv_pieces, biases)
    else:
        seqs = tokens.shape[0]
        every = lax.all_gather(coarse.reshape(tokens.shape), "seq", axis=1, tiled=True)
        keys = every.shape[1]
        every = every.reshape(-1, width)
        matrix = plan.gather(qkv_rows)
        ceilings = jnp.repeat(limits[:3].astype(BF16), width)[None]
        matrix = jnp.clip(matrix, -ceilings, ceilings)
        all_keys = jnp.clip(every, -limit_low, limit_low)
        clipped = jnp.clip(coarse, -limit_low, limit_low)
        queries = dots(clipped, matrix[:, :width], NN) + biases[:, :width]
        queries = queries.astype(BF16) * jnp.asarray(HD**-0.5, BF16)
        keys_values = (dots(all_keys, matrix[:, width:], NN) + biases[:, width:]).astype(BF16)
        cotangent_low = cotangent.astype(BF16).reshape(-1, width)
        rest_weights = [
            plan.gather(first_rows).reshape(plan.pairs, 2, -1, width + units),
            plan.gather(second_rows).reshape(plan.pairs, 2, -1, width),
        ]
    rows = coarse.shape[0] // seqs

    queries = queries.reshape(seqs, rows, width)
    keys_values = keys_values.reshape(seqs, keys, 2 * width)
    count = GROUP_PAIRS
    groups = range(0, width // LANES, count)
    contexts, inverses, weights = [], [], []
    for number, start in enumerate(groups):
        if number:
            queries, keys_values = after((queries, keys_values), contexts[-1])
        context, inverse, weight = attend(queries, keys_values, start, count)
        contexts.append(context)
        inverses.append(inverse)
        weights.append(weight)
    if plan.by_chip:
        rest_pieces[1:] = after(rest_pieces[1:], contexts[-1])
        rest_weights = plan.both_cores(rest_pieces)
    six = [bias_output, bias_down, gain_one, shift_one, gain_two, shift_two]
    six = jnp.stack(six + [jnp.zeros_like(bias_down)] * 2)
    result, grad_zero, context_grad, small, small_up, *grads = middle(
        here,
        [context.reshape(-1, count * LANES) for context in contexts],
        [inverse.reshape(-1, count * LANES) for inverse in inverses],
        coarse,
        cotangent_low,
        rest_weights,
        six,
        bias_up[None],
        (plan.pairs, plan.along),
    )
    layer_out = plan.to_home(result)
    mids = grads

    context_grad = context_grad.reshape(seqs, rows, width)
    chunks, sums = [], []
    for number, start in enumerate(groups):
        if plan.by_chip and number == 1:
            low = plan.add_cores(mids[0], mids[1], chunks[0][0])
            context_grad, low = after((context_grad, low))
            rest_sum = plan.total_pairs(low)
        if plan.by_chip and number == 2:
            context_grad, layer_out = after((context_grad, layer_out), chunks[1][0])
        grads = attend_back(queries, keys_values, contexts[number], context_grad, weights[number], start)
        chunks.append([grad.reshape(-1, count * LANES) for grad in grads[:3]])
        sums.append(jnp.sum(grads[3][:, :2], axis=0))
    terms = [(chunk[0], start * LANES) for chunk, start in zip(chunks, groups)]
    key_terms = [
        (chunk[kind], kind * width + start * LANES) for chunk, start in zip(chunks, groups) for kind in (1, 2)
    ]
    local_rows = coarse.shape[0]
    if plan.by_chip:
        leaving = back_to_tokens(key_terms, matrix, local_rows, local_rows)
        arrived = plan.swap(leaving)
        mine, theirs = weight_grads(here, clip_limits, [coarse, other], after(chunks, leaving), plan.pairs)
        own_terms = terms + key_terms
    else:
        partial = back_to_tokens(key_terms, matrix, 0, seqs * keys).reshape(seqs, keys, width)
        arrived = lax.psum_scatter(partial, "seq", scatter_dimension=1, tiled=True).reshape(-1, width)
        own_terms = terms
    tokens_grad = back_to_tokens(own_terms, matrix, 0, local_rows, (clip_limits, arrived, grad_zero, coarse))
    if plan.by_chip:
        late = plan.total_along(plan.total_pairs(plan.add_cores(mine, theirs)))
        rest_grad = plan.total_along(after(rest_sum, tokens_grad))
        first_grad, second_grad = rest_grad[:, : width + units], rest_grad[:, width + units :]
        second_grad = jnp.concatenate(jnp.split(second_grad, units // width, axis=1), axis=0)
    else:
        late = [
            dots(left, jnp.concatenate([chunk[kind] for chunk in chunks], axis=1), TN)
            for kind, left in enumerate((clipped, all_keys, all_keys))
        ]
        late = plan.scatter(jnp.concatenate(late, axis=1))
        first_grad = plan.scatter(mids[0].reshape(width, -1)).astype(F32)
        second_grad = plan.scatter(mids[1].reshape(units, -1)).astype(F32)
    tokens_grad = plan.to_home(tokens_grad).astype(F32)

    eight = jnp.concatenate([jnp.concatenate(sums, axis=1), small[:6]])
    eight = eight.reshape(8, devices, -1).transpose(1, 0, 2).reshape(devices, -1)
    small = jnp.concatenate([eight, small_up.reshape(devices, -1)], axis=1)
    small = jnp.sum(lax.all_to_all(small, AXES, split_axis=0, concat_axis=0, tiled=True), axis=0)
    share = width // devices
    small = [small[share * i : share * (i + 1)] for i in range(8)] + [small[8 * share :]]
    small = [small[0], small[1], small[2], small[8], *small[3:8]]

    shares = [late[:, :width], late[:, width : 2 * width], late[:, 2 * width :]]
    shares += [first_grad[:, :width], first_grad[:, width:], second_grad]
    masked = [
        jnp.where(jnp.abs(matrices[number]) < limits[number], shares[number], 0.0) for number in range(6)
    ]
    return (
        layer_out.astype(F32),
        tokens_grad,
        *masked,
        *small,
    )


def solution(mesh):
    pairs, along = mesh.shape["batch"] // 2, mesh.shape["seq"]
    fine_mesh = Mesh(mesh.devices.reshape(pairs, 2, along), AXES)
    rows = P(("pair", "core"), "seq", None)
    matrix = P(AXES, None)
    vector = P(AXES)

    def whole(tokens, *rest):
        plan = Plan(pairs, along, tokens.shape[0] // (2 * pairs))

        def run(*args):
            return local(plan, *args)

        return jax.shard_map(
            run,
            mesh=fine_mesh,
            in_specs=(rows, rows) + (matrix,) * 6 + (vector,) * 9 + (P(),),
            out_specs=(rows, rows) + (matrix,) * 6 + (vector,) * 9,
            check_vma=False,
        )(tokens, *rest)

    return whole
```

```python
import jax
import jax.numpy as jnp
from jax import lax
from jax.experimental import pallas as pl
from jax.experimental.pallas import tpu as pltpu
from jax.sharding import Mesh, PartitionSpec as P

HD = 64
LANES = 128
NORM_EPS = 1e-12
AXES = ("pair", "core", "seq")
GROUPS = (2, 4)
BACK_GROUPS = (1, 5)
SHORT = pl.CostEstimate(flops=1, transcendentals=0, bytes_accessed=1)
F32 = jnp.float32
BF16 = jnp.bfloat16

NT = (((1,), (1,)), ((), ()))
NN = (((1,), (0,)), ((), ()))
TN = (((0,), (0,)), ((), ()))


def dots(left, right, dims):
    return lax.dot_general(left, right, dims, preferred_element_type=F32)


def rounded(values):
    return lax.reduce_precision(values, 8, 7)


def prepare(matrices, vectors):
    rows, width = matrices[0].shape
    units = matrices[4].shape[1]
    count, number_of = len(matrices), len(vectors)

    def kernel(*refs):
        matrix_refs, vector_refs = refs[:count], refs[count : count + number_of]
        front_ref, rest_ref, packed_ref = refs[count + number_of :]
        for number in range(3):
            front_ref[:, width * number : width * (number + 1)] = matrix_refs[number][...].astype(BF16)
        rest_ref[:, :width] = matrix_refs[3][...].astype(BF16)
        rest_ref[:, width : width + units] = matrix_refs[4][...].astype(BF16)
        for j in range(units // width):
            part = matrix_refs[5][rows * j : rows * (j + 1)]
            rest_ref[:, width + units + width * j : width + units + width * (j + 1)] = part.astype(BF16)
        packed_ref[...] = jnp.zeros_like(packed_ref)
        for number, ref in enumerate(vector_refs):
            packed_ref[number : number + 1, : ref.shape[1]] = ref[...].astype(BF16)
        lane = lax.broadcasted_iota(jnp.int32, (1, LANES), 1)
        row = jnp.zeros((1, LANES), F32)
        for number, ref in enumerate(matrix_refs):
            largest = jnp.full((1, LANES), jnp.max(jnp.abs(ref[...])), F32)
            high = rounded(largest)
            middle_term = rounded(largest - high)
            for i, term in enumerate((high, middle_term, largest - high - middle_term)):
                row = jnp.where(lane == count * i + number, term, row)
        packed_ref[number_of : number_of + 1] = row.astype(BF16)

    return pl.pallas_call(
        kernel,
        out_shape=[
            jax.ShapeDtypeStruct((rows, 3 * width), BF16),
            jax.ShapeDtypeStruct((rows, width + 2 * units), BF16),
            jax.ShapeDtypeStruct((16, LANES), BF16),
        ],
        compiler_params=pltpu.CompilerParams(vmem_limit_bytes=56 << 20),
        cost_estimate=SHORT,
    )(*matrices, *[vector[None] for vector in vectors])


def parcel(values, limit):
    seqs, rows, width = values.shape
    block = min(256, rows)

    def kernel(limit_ref, values_ref, *refs):
        outs, place_ref = refs[:seqs], refs[seqs]
        place = lax.axis_index("seq")
        place_ref[0] = place
        if limit is not None:
            edge = jnp.full((1, width), limit_ref[0], F32)
            near = rounded(edge)
            below = jnp.where(near < edge, near, rounded(near * (1.0 - 2.0**-8)))
            above = jnp.where(near < edge, rounded(near * (1.0 + 1.5 * 2.0**-8)), near)
        for number, out in enumerate(outs):
            part = values_ref[lax.rem(place + number, seqs)]
            if limit is not None:
                size = jnp.abs(part)
                coarse = rounded(size)
                coarse = jnp.where(size < edge, jnp.minimum(coarse, below), jnp.maximum(coarse, above))
                part = jnp.where(part < 0, -coarse, coarse)
            out[...] = part.astype(BF16)

    smem_spec = pl.BlockSpec(memory_space=pltpu.SMEM)
    *parts, place = pl.pallas_call(
        kernel,
        grid=(rows // block,),
        in_specs=[smem_spec, pl.BlockSpec((seqs, block, width), lambda i: (0, i, 0))],
        out_specs=[pl.BlockSpec((block, width), lambda i: (i, 0))] * seqs + [smem_spec],
        out_shape=[jax.ShapeDtypeStruct((rows, width), BF16)] * seqs + [jax.ShapeDtypeStruct((1,), jnp.int32)],
        compiler_params=pltpu.CompilerParams(vmem_limit_bytes=56 << 20),
        cost_estimate=SHORT,
    )(jnp.zeros((1,), F32) if limit is None else limit, values)
    return parts, place[0]


def unpack(parts):
    seqs = len(parts)
    rows, width = parts[0].shape
    block = min(256, rows)

    def kernel(*refs):
        place = lax.axis_index("seq")
        for number, ref in enumerate(refs[:seqs]):
            refs[seqs][lax.rem(place + number, seqs)] = ref[...].astype(F32)

    return pl.pallas_call(
        kernel,
        grid=(rows // block,),
        in_specs=[pl.BlockSpec((block, width), lambda i: (i, 0))] * seqs,
        out_specs=pl.BlockSpec((seqs, block, width), lambda i: (0, i, 0)),
        out_shape=jax.ShapeDtypeStruct((seqs, rows, width), F32),
        compiler_params=pltpu.CompilerParams(vmem_limit_bytes=56 << 20),
        cost_estimate=SHORT,
    )(*parts)


def project(limit, tokens, pieces, biases):
    rows, width = tokens[0].shape
    pairs, along, piece_rows, columns = pieces[0].shape
    block = min(512, rows)
    steps = rows // block

    def kernel(limit_ref, own_ref, other_ref, bias_ref, same_ref, across_ref, q_ref, kv_ref, matrix_ref, held, sems):
        step = pl.program_id(0)
        core, seq = lax.axis_index("core"), lax.axis_index("seq")
        matrix = held.reshape(width, columns)
        store = pltpu.make_async_copy(matrix, matrix_ref, sems.at[2 * pairs * along])

        @pl.when(step == 0)
        def _():
            loads = []
            for far in range(pairs):
                for number, (piece, half) in enumerate(((same_ref, core), (across_ref, 1 - core))):
                    for near in range(along):
                        place = held.at[far, half, seq ^ near]
                        sem = sems.at[(2 * far + number) * along + near]
                        loads.append(pltpu.make_async_copy(piece.at[far, near], place, sem))
            for copy in loads:
                copy.start()
            for copy in loads:
                copy.wait()
            slots = [slice(256 * number, 256 * (number + 1)) for number in range(width // 256)]
            for number in range(3):
                lanes = slice(width * number, width * (number + 1))
                largest = jnp.zeros((256, width), F32)
                for slot in slots:
                    largest = jnp.maximum(largest, jnp.abs(matrix[slot, lanes].astype(F32)))
                top = jnp.full((1, width), 0.5 * jnp.max(largest), F32).astype(BF16)
                for slot in slots:
                    matrix[slot, lanes] = jnp.maximum(jnp.minimum(matrix[slot, lanes], top), -top)
            store.start()

        top = jnp.full((1, width), limit_ref[0], F32).astype(BF16)

        def clipped(ref):
            return jnp.maximum(jnp.minimum(ref[...], top), -top)

        @pl.when(step < steps)
        def _():
            all_three = dots(clipped(own_ref), matrix[...], NN) + bias_ref[...]
            q_ref[...] = all_three[:, :width].astype(BF16) * jnp.asarray(HD**-0.5, BF16)
            kv_ref[...] = all_three[:, width:].astype(BF16)

        @pl.when(step >= steps)
        def _():
            kv_ref[...] = (dots(clipped(other_ref), matrix[:, width:], NN) + bias_ref[:, width:]).astype(BF16)

        @pl.when(step == 2 * steps - 1)
        def _():
            store.wait()

    any_spec = pl.BlockSpec(memory_space=pl.ANY)
    smem_spec = pl.BlockSpec(memory_space=pltpu.SMEM)
    return pl.pallas_call(
        kernel,
        grid=(2 * steps,),
        in_specs=[
            smem_spec,
            pl.BlockSpec((block, width), lambda i: (jnp.minimum(i, steps - 1), 0)),
            pl.BlockSpec((block, width), lambda i: (jnp.maximum(i - steps, 0), 0)),
            pl.BlockSpec((1, columns), lambda i: (0, 0)),
            any_spec,
            any_spec,
        ],
        out_specs=[
            pl.BlockSpec((block, width), lambda i: (jnp.minimum(i, steps - 1), 0)),
            pl.BlockSpec((block, 2 * width), lambda i: (i, 0)),
            any_spec,
        ],
        out_shape=[
            jax.ShapeDtypeStruct((rows, width), BF16),
            jax.ShapeDtypeStruct((2 * rows, 2 * width), BF16),
            jax.ShapeDtypeStruct((width, columns), BF16),
        ],
        scratch_shapes=[
            pltpu.VMEM((pairs, 2, along, piece_rows, columns), BF16),
            pltpu.SemaphoreType.DMA((2 * pairs * along + 1,)),
        ],
        compiler_params=pltpu.CompilerParams(vmem_limit_bytes=56 << 20),
        cost_estimate=SHORT,
    )(limit, tokens[0], tokens[1], biases, *pieces)


def attend(queries, keys_values, start, count, filled=None):
    seqs, rows, width = queries.shape
    keys = keys_values.shape[1]
    pairs = width // LANES
    block = min(256, rows)
    held = [] if filled is None else list(filled)

    def kernel(q_ref, k_ref, v_ref, *refs):
        o_ref, l_ref, p_ref, token_ref = refs[len(held) :]
        low = lax.broadcasted_iota(jnp.int32, (1, LANES), 1) < HD
        q = q_ref[0]
        outs, inverses = [], []
        for half in range(2):
            mine = low if half == 0 else ~low
            scores = dots(jnp.where(mine, q, jnp.zeros_like(q)), k_ref[0], NT)
            weights = jnp.exp(scores - jnp.max(scores, axis=-1, keepdims=True))
            inverse = 1.0 / jnp.sum(weights, axis=-1, keepdims=True)
            weights = weights.astype(BF16)
            p_ref[0, half] = weights
            outs.append(dots(weights, v_ref[0], NN) * inverse)
            inverses.append(inverse)
        o_ref[0] = jnp.where(low, outs[0], outs[1]).astype(BF16)
        l_ref[0] = jnp.where(low, inverses[0], inverses[1])
        token_ref[...] = jnp.zeros_like(token_ref)

    rows_spec = pl.BlockSpec((1, block, LANES), lambda s, p, i: (s, i, start + p))
    return pl.pallas_call(
        kernel,
        grid=(seqs, count, rows // block),
        in_specs=[
            rows_spec,
            pl.BlockSpec((1, keys, LANES), lambda s, p, i: (s, 0, start + p)),
            pl.BlockSpec((1, keys, LANES), lambda s, p, i: (s, 0, pairs + start + p)),
        ]
        + [pl.BlockSpec(memory_space=pl.ANY)] * len(held),
        out_specs=[
            rows_spec,
            rows_spec,
            pl.BlockSpec((1, 2, block, keys), lambda s, p, i: (s, start + p, i, 0)),
            pl.BlockSpec((8, LANES), lambda s, p, i: (0, 0)),
        ],
        out_shape=[
            jax.ShapeDtypeStruct((seqs, rows, width), BF16),
            jax.ShapeDtypeStruct((seqs, rows, width), F32),
            jax.ShapeDtypeStruct((seqs, 2 * pairs, rows, keys), BF16),
            jax.ShapeDtypeStruct((8, LANES), F32),
        ],
        input_output_aliases={3 + i: i for i in range(len(held))},
        compiler_params=pltpu.CompilerParams(vmem_limit_bytes=56 << 20),
        cost_estimate=SHORT,
    )(queries, keys_values, keys_values, *held)


def attend_back(queries, keys_values, context, inverse, context_grad, weights, start, count, filled=None):
    seqs, rows, width = queries.shape
    keys = keys_values.shape[1]
    pairs = width // LANES
    block = min(512, rows)
    held = [] if filled is None else list(filled)

    def kernel(q_ref, k_ref, v_ref, o_ref, l_ref, do_ref, p_ref, *refs):
        dq_ref, dk_ref, dv_ref, sums_ref, token_ref, dk_sum, dv_sum = refs[len(held) :]
        step = pl.program_id(2)
        low = lax.broadcasted_iota(jnp.int32, (1, LANES), 1) < HD
        q, do = q_ref[0], (do_ref[0].astype(F32) * l_ref[0]).astype(BF16)
        product = do.astype(F32) * o_ref[0].astype(F32)
        q_turned, do_turned = q.T, do.T

        @pl.when(step == 0)
        def _():
            dk_sum[...] = jnp.zeros_like(dk_sum)
            dv_sum[...] = jnp.zeros_like(dv_sum)
            sums_ref[...] = jnp.zeros_like(sums_ref)
            token_ref[...] = jnp.zeros_like(token_ref)

        grads = []
        for half in range(2):
            mine = low if half == 0 else ~low
            lanes = slice(half * HD, (half + 1) * HD)
            delta = jnp.sum(jnp.where(mine, product, 0.0), axis=-1, keepdims=True)
            raised = dots(jnp.where(mine, do, jnp.zeros_like(do)), v_ref[0], NT)
            p = p_ref[0, half]
            ds = (raised - delta).astype(BF16) * p
            grads.append(dots(ds, k_ref[0], NN))
            dk_sum[lanes] += dots(q_turned[lanes], ds, NN)
            dv_sum[lanes] += dots(do_turned[lanes], p, NN)
        dq = (jnp.where(low, grads[0], grads[1]) * HD**-0.5).astype(BF16)
        dq_ref[0] = dq
        sums_ref[0, 0:1] += jnp.sum(dq.astype(F32), axis=0, keepdims=True)

        @pl.when(step == pl.num_programs(2) - 1)
        def _():
            dk_ref[0] = dk_sum[...].T.astype(BF16)
            dv = dv_sum[...].T.astype(BF16)
            dv_ref[0] = dv
            sums_ref[0, 1:2] = jnp.sum(dv.astype(F32), axis=0, keepdims=True)

    rows_spec = pl.BlockSpec((1, block, LANES), lambda s, p, i: (s, i, start + p))
    keys_spec = pl.BlockSpec((1, keys, LANES), lambda s, p, i: (s, 0, start + p))
    return pl.pallas_call(
        kernel,
        grid=(seqs, count, rows // block),
        in_specs=[
            rows_spec,
            keys_spec,
            pl.BlockSpec((1, keys, LANES), lambda s, p, i: (s, 0, pairs + start + p)),
            rows_spec,
            rows_spec,
            rows_spec,
            pl.BlockSpec((1, 2, block, keys), lambda s, p, i: (s, start + p, i, 0)),
        ]
        + [pl.BlockSpec(memory_space=pl.ANY)] * len(held),
        out_specs=[
            rows_spec,
            keys_spec,
            keys_spec,
            pl.BlockSpec((1, 8, LANES), lambda s, p, i: (s, 0, start + p)),
            pl.BlockSpec((8, LANES), lambda s, p, i: (0, 0)),
        ],
        out_shape=[
            jax.ShapeDtypeStruct((seqs, rows, width), BF16),
            jax.ShapeDtypeStruct((seqs, keys, width), BF16),
            jax.ShapeDtypeStruct((seqs, keys, width), BF16),
            jax.ShapeDtypeStruct((seqs, 8, width), F32),
            jax.ShapeDtypeStruct((8, LANES), F32),
        ],
        input_output_aliases={7 + i: i for i in range(len(held))},
        scratch_shapes=[pltpu.VMEM((LANES, keys), F32), pltpu.VMEM((LANES, keys), F32)],
        compiler_params=pltpu.CompilerParams(vmem_limit_bytes=56 << 20),
        cost_estimate=SHORT,
    )(queries, keys_values, keys_values, context, inverse, context_grad, weights, *held)


def back_to_tokens(terms, matrix, first_row, rows, finish=None):
    width, columns = matrix.shape
    block = min(512, rows)
    shift = first_row // block
    extra = [] if finish is None else list(finish)

    def kernel(*refs):
        matrix_ref, parts, refs = refs[0], refs[1 : 1 + len(terms)], refs[1 + len(terms) :]
        total = None
        for ref, (part, column) in zip(parts, terms):
            product = dots(ref[...], matrix_ref[:, column : column + part.shape[1]], NT)
            total = product if total is None else total + product
        if finish is not None:
            limit_ref, arrived_ref, zero_ref, tokens_ref, out_ref = refs
            total = total + arrived_ref[...].astype(F32)
            inside = jnp.abs(tokens_ref[...].astype(F32)) < limit_ref[0]
            total = zero_ref[...].astype(F32) + jnp.where(inside, total, 0.0)
        else:
            (out_ref,) = refs
        out_ref[...] = total.astype(BF16)

    row_spec = pl.BlockSpec((block, width), lambda i: (i, 0))
    return pl.pallas_call(
        kernel,
        grid=(rows // block,),
        in_specs=[pl.BlockSpec((width, columns), lambda i: (0, 0), pipeline_mode=pl.Buffered(1))]
        + [pl.BlockSpec((block, part.shape[1]), lambda i: (shift + i, 0)) for part, _ in terms]
        + ([] if finish is None else [pl.BlockSpec(memory_space=pltpu.SMEM)] + [row_spec] * 3),
        out_specs=row_spec,
        out_shape=jax.ShapeDtypeStruct((rows, width), BF16),
        compiler_params=pltpu.CompilerParams(vmem_limit_bytes=56 << 20),
        cost_estimate=SHORT,
    )(matrix, *[part for part, _ in terms], *extra)


def weight_grads(limit, tokens, chunks, sums, shape):
    rows, width = tokens[0].shape
    block = min(512, rows)
    steps = rows // block
    spans = [chunk[0].shape[1] for chunk in chunks]
    columns = 3 * width + LANES
    pairs, along = shape
    piece_rows = width // (2 * pairs * along)

    def kernel(limit_ref, own_ref, other_ref, sums_ref, *refs):
        grads, (mine_ref, theirs_ref, total, held, sems) = refs[: 3 * len(chunks)], refs[3 * len(chunks) :]
        step = pl.program_id(0)
        core = lax.axis_index("core")
        top = jnp.full((1, width), limit_ref[0], F32).astype(BF16)

        @pl.when(step == 0)
        def _():
            total[...] = jnp.zeros_like(total)

        def add(tokens_ref, kinds):
            turned = jnp.maximum(jnp.minimum(tokens_ref[...], top), -top).T
            for number, span in enumerate(spans):
                for kind in kinds:
                    start = width * kind + sum(spans[:number])
                    total[:, start : start + span] += dots(turned, grads[3 * number + kind][...], NN)

        @pl.when(step < steps)
        def _():
            add(own_ref, (0, 1, 2))

        @pl.when(step >= steps)
        def _():
            add(other_ref, (1, 2))

        @pl.when(step == 2 * steps - 1)
        def _():
            part = held.shape[:-1]
            held[..., : 3 * width] = total[...].astype(BF16).reshape(part + (3 * width,))
            rows_of = jnp.concatenate([sums_ref[...], jnp.zeros((LANES - sums_ref.shape[0], width), F32)], axis=0)
            held[..., 3 * width :] = rows_of.T.astype(BF16).reshape(part + (LANES,))
            stores = []
            for far in range(pairs):
                for number, (target, half) in enumerate(((mine_ref, core), (theirs_ref, 1 - core))):
                    stores.append(pltpu.make_async_copy(held.at[far, half], target.at[far], sems.at[2 * far + number]))
            for copy in stores:
                copy.start()
            for copy in stores:
                copy.wait()

    smem_spec = pl.BlockSpec(memory_space=pltpu.SMEM)

    def specs(span):
        own_spec = pl.BlockSpec((block, span), lambda i: (jnp.minimum(i, steps - 1), 0))
        return [own_spec] + [pl.BlockSpec((block, span), lambda i: (i, 0))] * 2

    part = jax.ShapeDtypeStruct((pairs, along, piece_rows, columns), BF16)
    return pl.pallas_call(
        kernel,
        grid=(2 * steps,),
        in_specs=[
            smem_spec,
            pl.BlockSpec((block, width), lambda i: (jnp.minimum(i, steps - 1), 0)),
            pl.BlockSpec((block, width), lambda i: (jnp.maximum(i - steps, 0), 0)),
            pl.BlockSpec(sums.shape, lambda i: (0, 0)),
        ]
        + [spec for span in spans for spec in specs(span)],
        out_specs=[pl.BlockSpec(memory_space=pl.ANY)] * 2,
        out_shape=[part, part],
        scratch_shapes=[
            pltpu.VMEM((width, 3 * width), F32),
            pltpu.VMEM((pairs, 2, along, piece_rows, columns), BF16),
            pltpu.SemaphoreType.DMA((2 * pairs,)),
        ],
        compiler_params=pltpu.CompilerParams(vmem_limit_bytes=56 << 20),
        cost_estimate=SHORT,
    )(limit, tokens[0], tokens[1], sums, *[grad for chunk in chunks for grad in chunk])


def middle(context, residual, cotangent, weights, vectors, up_bias, shape):
    rows, width = residual.shape
    units = up_bias.shape[1]
    pairs, along = shape
    block = min(512, rows)
    blocks = units // width
    parts = len(weights)
    whole = parts == 2
    share = width // (2 * pairs * along)
    if whole:
        first_shape = (pairs, 2, along * share, width + units)
        second_shape = (pairs, 2, along * share * blocks, width)
    else:
        first_shape = (pairs, 2, along, share, width + units)
        second_shape = (pairs, 2, along, blocks, share, width)
    copies = 2 if whole else 2 * pairs * (1 + blocks)

    def kernel(residual_ref, cot_ref, vector_ref, bias_ref, *refs):
        context_ref, refs = refs[0], refs[1:]
        weight_refs, refs = refs[:parts], refs[parts:]
        result_ref, zero_ref, back_ref, packed_ref, *outs, small_ref, small_up_ref, first, second, grad_output, grad_up, grad_down = refs[:-3]
        act_ref, slope_ref, sems = refs[-3:]
        step = pl.program_id(0)
        pair, core = lax.axis_index("pair"), lax.axis_index("core")

        def matches(pieces):
            if whole:
                return [(pieces[0], first), (pieces[1], second)]
            found = []
            for piece, place, half in pieces:
                found.append((piece.at[:, :, : width + units], first.at[place, half]))
                for j in range(blocks):
                    lanes = slice(width + units + width * j, width + units + width * (j + 1))
                    found.append((piece.at[:, :, lanes], second.at[place, half].at[:, j]))
            return found

        halves = core, 1 - core
        if whole:
            sources, targets = weight_refs, outs
        else:
            sources = [(ref, pair ^ (i // 2), halves[i % 2]) for i, ref in enumerate(weight_refs)]
            targets = [(out.at[far], pair ^ far, half) for far in range(pairs) for out, half in zip(outs, halves)]
        loads = [
            pltpu.make_async_copy(outside, place, sems.at[i]) for i, (outside, place) in enumerate(matches(sources))
        ]

        @pl.when(step == 0)
        def _():
            for copy in loads:
                copy.start()
            small_ref[...] = jnp.zeros_like(small_ref)
            small_up_ref[...] = jnp.zeros_like(small_up_ref)
            grad_output[...] = jnp.zeros_like(grad_output)
            grad_up[...] = jnp.zeros_like(grad_up)
            grad_down[...] = jnp.zeros_like(grad_down)
            for copy in loads:
                copy.wait()

        def vector(number):
            return vector_ref[number : number + 1]

        def mean(values):
            return jnp.mean(values, axis=-1, keepdims=True)

        def columns(j):
            return slice(width * j, width * (j + 1))

        def output_matrix():
            return first[(..., slice(0, width))].reshape(width, width)

        def up_matrix(j):
            return first[(..., slice(width * (j + 1), width * (j + 2)))].reshape(width, width)

        down_rows = second.reshape(units, width)

        bias_output, bias_down, gain_one, shift_one, gain_two, shift_two = [vector(i) for i in range(6)]
        ctx = context_ref[...]
        zero = residual_ref[...].astype(F32) + dots(ctx, output_matrix(), NN) + bias_output
        center = zero - mean(zero)
        scale_one = lax.rsqrt(mean(center * center) + NORM_EPS)
        normal_one = center * scale_one
        hidden = normal_one * gain_one + shift_one
        hidden_low = hidden.astype(BF16)
        summed = hidden + bias_down
        for j in range(blocks):
            up = dots(hidden_low, up_matrix(j), NN) + bias_ref[:, columns(j)]
            below = 0.5 + 0.5 * lax.erf(up * 0.7071067811865476)
            act = (up * below).astype(BF16)
            act_ref[:, columns(j)] = act
            slope = below + up * (0.3989422804014327 * jnp.exp(-0.5 * up * up))
            slope_ref[:, columns(j)] = slope.astype(BF16)
            summed = summed + dots(act, down_rows[columns(j)], NN)
        center = summed - mean(summed)
        scale_two = lax.rsqrt(mean(center * center) + NORM_EPS)
        normal_two = center * scale_two
        result_ref[...] = (normal_two * gain_two + shift_two).astype(result_ref.dtype)

        cot = cot_ref[...].astype(F32)
        scaled = cot * gain_two
        grad_summed = scale_two * (scaled - mean(scaled) - normal_two * mean(scaled * normal_two))
        down_low = grad_summed.astype(BF16)
        grad_hidden = grad_summed
        for j in range(blocks):
            lifted = dots(down_low, down_rows[columns(j)], NT) * slope_ref[:, columns(j)].astype(F32)
            up_low = lifted.astype(BF16)
            small_up_ref[:, columns(j)] += jnp.sum(up_low.astype(F32), axis=0, keepdims=True)
            grad_up[:, columns(j)] += dots(hidden_low, up_low, TN)
            grad_hidden = grad_hidden + dots(up_low, up_matrix(j), NT)
            grad_down[columns(j)] += dots(act_ref[:, columns(j)], down_low, TN)
        scaled = grad_hidden * gain_one
        grad_zero = scale_one * (scaled - mean(scaled) - normal_one * mean(scaled * normal_one))
        branch_low = grad_zero.astype(BF16)
        zero_ref[...] = branch_low
        grad_output[...] += dots(ctx, branch_low, TN)
        back_ref[...] = dots(branch_low, output_matrix(), NT).astype(BF16)
        sums = [branch_low.astype(F32), down_low.astype(F32), grad_hidden * normal_one, grad_hidden, cot * normal_two, cot]
        for number, terms in enumerate(sums):
            small_ref[number : number + 1] += jnp.sum(terms, axis=0, keepdims=True)

        @pl.when(step == pl.num_programs(0) - 1)
        def _():
            part = first.shape[:-1] + (width,)
            first[(..., slice(0, width))] = grad_output[...].astype(BF16).reshape(part)
            for j in range(blocks):
                lanes = slice(width * (j + 1), width * (j + 2))
                first[(..., lanes)] = grad_up[:, columns(j)].astype(BF16).reshape(part)
            second[...] = grad_down[...].astype(BF16).reshape(second.shape)
            stores = [
                pltpu.make_async_copy(place, outside, sems.at[i]) for i, (outside, place) in enumerate(matches(targets))
            ]
            for copy in stores:
                copy.start()
            packed_ref[...] = jnp.zeros_like(packed_ref)
            for device in range(2 * pairs * along):
                packed_ref[device, :8, :share] = small_ref[:, share * device : share * (device + 1)]
                up_lanes = slice(share * blocks * device, share * blocks * (device + 1))
                packed_ref[device, 8:9, : share * blocks] = small_up_ref[:, up_lanes]
            for copy in stores:
                copy.wait()

    any_spec = pl.BlockSpec(memory_space=pl.ANY)
    row_spec = pl.BlockSpec((block, width), lambda i: (i, 0))
    if whole:
        grads = [jax.ShapeDtypeStruct(first_shape, BF16), jax.ShapeDtypeStruct(second_shape, BF16)]
    else:
        grads = [jax.ShapeDtypeStruct((pairs, along, share, width + 2 * units), BF16)] * 2
    return pl.pallas_call(
        kernel,
        grid=(rows // block,),
        in_specs=[row_spec] * 2
        + [pl.BlockSpec((8, width), lambda i: (0, 0)), pl.BlockSpec((1, units), lambda i: (0, 0))]
        + [row_spec]
        + [any_spec] * parts,
        out_specs=[row_spec] * 3
        + [pl.BlockSpec((2 * pairs * along, 16, LANES), lambda i: (0, 0, 0))]
        + [any_spec] * 2,
        out_shape=[
            jax.ShapeDtypeStruct((rows, width), BF16),
            jax.ShapeDtypeStruct((rows, width), BF16),
            jax.ShapeDtypeStruct((rows, width), BF16),
            jax.ShapeDtypeStruct((2 * pairs * along, 16, LANES), F32),
            *grads,
        ],
        scratch_shapes=[
            pltpu.VMEM((8, width), F32),
            pltpu.VMEM((1, units), F32),
            pltpu.VMEM(first_shape, BF16),
            pltpu.VMEM(second_shape, BF16),
            pltpu.VMEM((width, width), F32),
            pltpu.VMEM((width, units), F32),
            pltpu.VMEM((units, width), F32),
            pltpu.VMEM((block, units), BF16),
            pltpu.VMEM((block, units), BF16),
            pltpu.SemaphoreType.DMA((copies,)),
        ],
        compiler_params=pltpu.CompilerParams(vmem_limit_bytes=62 << 20),
        cost_estimate=SHORT,
    )(residual, cotangent, vectors, up_bias, context, *weights)


def after(values, *earlier):
    return lax.optimization_barrier((values, earlier))[0]


class Plan:
    def __init__(self, pairs, along, seqs):
        self.pairs, self.along, self.seqs = pairs, along, seqs
        self.devices = 2 * pairs * along
        self.by_chip = 2 * seqs == along and pairs == 4 and along & (along - 1) == 0

    def moves(self, number):
        table = []
        for pair in range(self.pairs):
            for core in range(2):
                for place in range(self.along):
                    source = (pair * 2 + core) * self.along + place
                    chip = core * self.seqs + (place + number) % self.seqs
                    target = (pair * 2 + 1 - place // self.seqs) * self.along + chip
                    table.append((source, target))
        return table

    def send(self, part, number, *earlier):
        return lax.ppermute(after(part, *earlier), AXES, self.moves(number))

    def send_home(self, worked):
        blocks = worked.reshape(self.seqs, -1, worked.shape[-1])
        if not self.by_chip:
            return blocks
        return [
            lax.ppermute(blocks[number], AXES, [(b, a) for a, b in self.moves(number)]) for number in range(self.seqs)
        ]

    def at_home(self, back):
        return unpack(back) if self.by_chip else back.astype(F32)

    def swap(self, values):
        return lax.ppermute(values, "core", [(0, 1), (1, 0)])

    def meet(self, values, axis, far):
        count = lax.axis_size(axis)
        return lax.ppermute(values, axis, [(i, i ^ far) for i in range(count)])

    def column(self, rows, *earlier):
        return [rows] + after([self.meet(rows, "seq", far) for far in range(1, self.along)], *earlier)

    def ordered(self, column, here):
        held = jnp.zeros((self.along,) + column[0].shape, column[0].dtype)
        for far in range(self.along):
            held = lax.dynamic_update_index_in_dim(held, column[far], here ^ far, 0)
        return held

    def both_cores(self, pieces):
        return [part for piece in pieces for part in (piece, self.swap(piece))]

    def add_cores(self, mine, theirs, *earlier):
        theirs = after(self.swap(theirs), *earlier)
        return (mine.astype(F32) + theirs.astype(F32)).astype(BF16)

    def add_blocks(self, mine, theirs, *earlier):
        theirs = after(self.swap(theirs), *earlier)
        return [(mine[far].astype(F32) + theirs[far].astype(F32)).astype(BF16) for far in range(self.pairs)]

    def spread(self, column):
        copies = jnp.broadcast_to(column[None], (self.pairs,) + column.shape)
        return lax.all_to_all(copies, "pair", split_axis=0, concat_axis=0, tiled=True)

    def near_and_far(self, column):
        return [column] + [self.meet(column, "pair", far) for far in range(1, self.pairs)]

    def total_along(self, values, *earlier):
        return self.gathered(values, "seq", *earlier)

    def gathered(self, parts, axis, *earlier):
        arrived = after([self.meet(parts[far], axis, far) for far in range(1, len(parts))], *earlier)
        total = parts[0].astype(F32)
        for part in arrived:
            total = total + part.astype(F32)
        return total

    def total(self, parts, axis):
        arrived = lax.all_to_all(parts, axis, split_axis=0, concat_axis=0, tiled=True)
        return jnp.sum(arrived.astype(F32), axis=0)

    def everywhere(self, values):
        copies = jnp.broadcast_to(values[None], (self.devices,) + values.shape)
        return lax.all_to_all(copies, AXES, split_axis=0, concat_axis=0, tiled=True)

    def exchange(self, parts):
        return lax.all_to_all(parts, AXES, split_axis=0, concat_axis=0, tiled=True)

    def gather(self, rows):
        return lax.all_gather(rows, AXES, axis=0, tiled=True)

    def scatter(self, total):
        return lax.psum_scatter(total, AXES, scatter_dimension=0, tiled=True)


def local(plan, tokens, cotangent, *rest):
    params, clip_limits = rest[:15], rest[15]
    limit = clip_limits[0]
    matrices = params[:6]
    width = tokens.shape[-1]
    units = matrices[4].shape[1]
    devices = plan.devices

    chosen, place = parcel(tokens, clip_limits)
    if plan.by_chip:
        qkv_rows, rest_rows, packed = prepare(matrices, params[6:])
        qkv_column = jnp.stack(plan.column(qkv_rows))
        vectors = plan.everywhere(packed)
        coarse = jnp.concatenate([plan.send(part, i, vectors) for i, part in enumerate(chosen)], axis=0)
        vectors = vectors.astype(F32)
        sizes = [vector.shape[0] for vector in params[6:]]
        vectors, terms = [vectors[:, i, :size].reshape(-1) for i, size in enumerate(sizes)], vectors[:, len(sizes), :18]
        limits = 0.5 * jnp.max(terms[:, :6] + terms[:, 6:12] + terms[:, 12:18], axis=0)
    else:
        coarse = jnp.roll(jnp.stack(chosen), place, axis=0).reshape(-1, width)
        vectors = [lax.all_gather(vector.astype(BF16), AXES, axis=0, tiled=True).astype(F32) for vector in params[6:]]
        limits = 0.5 * lax.pmax(jnp.stack([jnp.max(jnp.abs(matrix)) for matrix in matrices]), AXES)
    bias_query, bias_value, bias_output, bias_up, bias_down, gain_one, shift_one, gain_two, shift_two = vectors
    biases = jnp.concatenate([bias_query, jnp.zeros_like(bias_value), bias_value])[None]
    limit_low = limit.astype(BF16)

    def clip_to(number):
        return jnp.clip(matrices[number], -limits[number], limits[number]).astype(BF16)

    if plan.by_chip:
        seqs, keys = 1, 2 * coarse.shape[0]
        chosen_cotangent = parcel(after(cotangent, chosen), None)[0]
        ceilings = [jnp.full((size,), top, BF16) for size, top in zip((width, units, units), limits[3:].astype(BF16))]
        ceilings = jnp.concatenate(ceilings)[None, None]
        rest_column = plan.ordered(plan.column(after(rest_rows, qkv_column)), place)
        rest_column = jnp.clip(rest_column, -ceilings, ceilings)
        rest_pieces = plan.near_and_far(rest_column)
        qkv_same = plan.spread(qkv_column)
        qkv_across = plan.swap(qkv_same)
        coarse, chosen_cotangent = after((coarse, chosen_cotangent), rest_column, qkv_across)
        other = plan.swap(coarse)
        queries, keys_values, matrix = project(clip_limits, [coarse, other], [qkv_same, qkv_across], biases)
        cotangent_low = [plan.send(chosen_cotangent[0], 0)]
        cotangent_low += [plan.send(part, i + 1, queries) for i, part in enumerate(chosen_cotangent[1:])]
    else:
        seqs = tokens.shape[0]
        every = lax.all_gather(coarse.reshape(tokens.shape), "seq", axis=1, tiled=True)
        keys = every.shape[1]
        every = every.reshape(-1, width)
        matrix = plan.gather(jnp.concatenate([matrix.astype(BF16) for matrix in matrices[:3]], axis=1))
        ceilings = jnp.repeat(limits[:3].astype(BF16), width)[None]
        matrix = jnp.clip(matrix, -ceilings, ceilings)
        all_keys = jnp.clip(every, -limit_low, limit_low)
        clipped = jnp.clip(coarse, -limit_low, limit_low)
        queries = dots(clipped, matrix[:, :width], NN) + biases[:, :width]
        queries = queries.astype(BF16) * jnp.asarray(HD**-0.5, BF16)
        keys_values = (dots(all_keys, matrix[:, width:], NN) + biases[:, width:]).astype(BF16)
        cotangent_low = cotangent.astype(BF16).reshape(-1, width)
        rest_weights = [
            plan.gather(jnp.concatenate([clip_to(3), clip_to(4)], axis=1)).reshape(plan.pairs, 2, -1, width + units),
            plan.gather(clip_to(5)).reshape(plan.pairs, 2, -1, width),
        ]
    rows = coarse.shape[0] // seqs

    queries = queries.reshape(seqs, rows, width)
    keys_values = keys_values.reshape(seqs, keys, 2 * width)
    filled = None
    for number, count in enumerate(GROUPS):
        *filled, token = attend(queries, keys_values, sum(GROUPS[:number]), count, filled)
        queries, keys_values = after((queries, keys_values), token)
    if plan.by_chip:
        cotangent_low = jnp.concatenate(cotangent_low, axis=0)
        rest_pieces = after(rest_pieces, token, cotangent_low)
        rest_weights = plan.both_cores(rest_pieces)
    context, inverse, weights = filled
    six = [bias_output, bias_down, gain_one, shift_one, gain_two, shift_two]
    six = jnp.stack(six + [jnp.zeros_like(bias_down)] * 2)
    result, grad_zero, context_grad, small, *grads = middle(
        context.reshape(-1, width),
        coarse,
        cotangent_low,
        rest_weights,
        six,
        bias_up[None],
        (plan.pairs, plan.along),
    )
    layer_out = result if plan.by_chip else plan.send_home(result)
    mids = grads
    small = plan.exchange(small)

    context_grad = context_grad.reshape(seqs, rows, width)
    filled = None
    for number, count in enumerate(BACK_GROUPS):
        *filled, token = attend_back(
            queries, keys_values, context, inverse, context_grad, weights, sum(BACK_GROUPS[:number]), count, filled
        )
        if plan.by_chip and number == 0:
            low = plan.add_blocks(mids[0], mids[1], token)
            context_grad, low = after((context_grad, low))
            rest_sum = plan.gathered(low, "pair").astype(BF16)
            layer_out = plan.send_home(after(result, token))
        context_grad = after(context_grad, token)
    grads = [grad.reshape(-1, width) for grad in filled[:3]]
    sums = jnp.sum(filled[3], axis=0)
    key_terms = [(grads[1], width), (grads[2], 2 * width)]
    local_rows = coarse.shape[0]
    if plan.by_chip:
        mine, theirs = weight_grads(clip_limits, [coarse, other], [grads], sums, (plan.pairs, plan.along))
        layer_out, rest_sum, matrix, small = after((layer_out, rest_sum, matrix, small), mine)
        rest_sum = [
            lax.dynamic_index_in_dim(rest_sum, place ^ far, 0, keepdims=False) for far in range(plan.along)
        ]
        rest_sum, matrix = after((rest_sum, matrix))
        leaving = back_to_tokens(key_terms, matrix, local_rows, local_rows)
        arrived = plan.swap(leaving)
        late = plan.add_cores(mine, theirs)
        arrived, late = after((arrived, late))
        own_terms = [(grads[0], 0)] + key_terms
    else:
        partial = back_to_tokens(key_terms, matrix, 0, seqs * keys).reshape(seqs, keys, width)
        arrived = lax.psum_scatter(partial, "seq", scatter_dimension=1, tiled=True).reshape(-1, width)
        own_terms = [(grads[0], 0)]
    tokens_grad = back_to_tokens(own_terms, matrix, 0, local_rows, (clip_limits, arrived, grad_zero, coarse))
    if plan.by_chip:
        late = plan.total(late, "pair").astype(BF16)
        rest_parts = after([plan.meet(rest_sum[far], "seq", far) for far in range(1, plan.along)], tokens_grad)
        tokens_grad, rest_parts, late = after((tokens_grad, rest_parts, late))
        rest_grad = rest_sum[0].astype(F32)
        for part in rest_parts:
            rest_grad = rest_grad + part.astype(F32)
        late = plan.total(late, "seq")
        layer_out = after(layer_out, tokens_grad)
        bias_grads = [late[:, 3 * width + i] for i in range(2)]
        first_grad, second_grad = rest_grad[:, : width + units], rest_grad[:, width + units :]
        second_grad = jnp.concatenate(jnp.split(second_grad, units // width, axis=1), axis=0)
    else:
        late = [
            dots(left, grads[kind], TN) for kind, left in enumerate((clipped, all_keys, all_keys))
        ]
        late = plan.scatter(jnp.concatenate(late, axis=1))
        bias_grads = [plan.scatter(sums[i]) for i in range(2)]
        first_grad = plan.scatter(mids[0].reshape(width, -1)).astype(F32)
        second_grad = plan.scatter(mids[1].reshape(units, -1)).astype(F32)
    tokens_grad = plan.at_home(plan.send_home(tokens_grad))
    small = jnp.sum(after(small, tokens_grad), axis=0)
    small_up = small[8, : units // devices]
    share = width // devices
    small = [small[i, :share] for i in range(6)]
    small = [*bias_grads, small[0], small_up, *small[1:]]

    shares = [late[:, :width], late[:, width : 2 * width], late[:, 2 * width : 3 * width]]
    shares += [first_grad[:, :width], first_grad[:, width:], second_grad]
    masked = [
        jnp.where(jnp.abs(matrices[number]) < limits[number], shares[number], 0.0) for number in range(6)
    ]
    return (
        plan.at_home(layer_out),
        tokens_grad,
        *masked,
        *small,
    )


def solution(mesh):
    pairs, along = mesh.shape["batch"] // 2, mesh.shape["seq"]
    fine_mesh = Mesh(mesh.devices.reshape(pairs, 2, along), AXES)
    rows = P(("pair", "core"), "seq", None)
    matrix = P(AXES, None)
    vector = P(AXES)

    def whole(tokens, *rest):
        plan = Plan(pairs, along, tokens.shape[0] // (2 * pairs))

        def run(*args):
            return local(plan, *args)

        return jax.shard_map(
            run,
            mesh=fine_mesh,
            in_specs=(rows, rows) + (matrix,) * 6 + (vector,) * 9 + (P(),),
            out_specs=(rows, rows) + (matrix,) * 6 + (vector,) * 9,
            check_vma=False,
        )(tokens, *rest)

    return whole
```

```python
import jax
import jax.numpy as jnp
from jax import lax
from jax.experimental import pallas as pl
from jax.experimental.pallas import tpu as pltpu
from jax.sharding import Mesh, PartitionSpec as P

HD = 64
LANES = 128
NORM_EPS = 1e-12
SAFE_SCORE = 60.0
AXES = ("pair", "core", "seq")
GROUPS = (2, 4)
BACK_GROUPS = (1, 5)
SHORT = pl.CostEstimate(flops=1, transcendentals=0, bytes_accessed=1)
F32 = jnp.float32
BF16 = jnp.bfloat16

NT = (((1,), (1,)), ((), ()))
NN = (((1,), (0,)), ((), ()))
TN = (((0,), (0,)), ((), ()))


def dots(left, right, dims):
    return lax.dot_general(left, right, dims, preferred_element_type=F32)


def rounded(values):
    return lax.reduce_precision(values, 8, 7)


def prepare(matrices, vectors):
    rows, width = matrices[0].shape
    units = matrices[4].shape[1]
    count, number_of = len(matrices), len(vectors)

    def kernel(*refs):
        matrix_refs, vector_refs = refs[:count], refs[count : count + number_of]
        front_ref, rest_ref, packed_ref = refs[count + number_of :]
        for number in range(3):
            front_ref[:, width * number : width * (number + 1)] = matrix_refs[number][...].astype(BF16)
        rest_ref[:, :width] = matrix_refs[3][...].astype(BF16)
        rest_ref[:, width : width + units] = matrix_refs[4][...].astype(BF16)
        for j in range(units // width):
            part = matrix_refs[5][rows * j : rows * (j + 1)]
            rest_ref[:, width + units + width * j : width + units + width * (j + 1)] = part.astype(BF16)
        packed_ref[...] = jnp.zeros_like(packed_ref)
        for number, ref in enumerate(vector_refs):
            packed_ref[number : number + 1, : ref.shape[1]] = ref[...].astype(BF16)
        lane = lax.broadcasted_iota(jnp.int32, (1, LANES), 1)
        row = jnp.zeros((1, LANES), F32)
        for number, ref in enumerate(matrix_refs):
            largest = jnp.full((1, LANES), jnp.max(jnp.abs(ref[...])), F32)
            high = rounded(largest)
            middle_term = rounded(largest - high)
            for i, term in enumerate((high, middle_term, largest - high - middle_term)):
                row = jnp.where(lane == count * i + number, term, row)
        packed_ref[number_of : number_of + 1] = row.astype(BF16)

    return pl.pallas_call(
        kernel,
        out_shape=[
            jax.ShapeDtypeStruct((rows, 3 * width), BF16),
            jax.ShapeDtypeStruct((rows, width + 2 * units), BF16),
            jax.ShapeDtypeStruct((16, LANES), BF16),
        ],
        compiler_params=pltpu.CompilerParams(vmem_limit_bytes=56 << 20),
        cost_estimate=SHORT,
    )(*matrices, *[vector[None] for vector in vectors])


def head_lengths(rows):
    width = rows.shape[1]
    feature = lax.broadcasted_iota(jnp.int32, (width, LANES), 0)
    head = lax.broadcasted_iota(jnp.int32, (width, LANES), 1)
    members = jnp.where((feature >= head * HD) & (feature < (head + 1) * HD), 1.0, 0.0).astype(BF16)
    wide = rows.astype(F32)
    return jnp.max(dots((wide * wide).astype(BF16), members, NN), axis=0, keepdims=True)


def parcel(values, limit):
    seqs, rows, width = values.shape
    block = min(256, rows)

    def kernel(limit_ref, values_ref, *refs):
        outs, place_ref = refs[:seqs], refs[seqs]
        place = lax.axis_index("seq")
        place_ref[0] = place
        if limit is not None:
            edge = jnp.full((1, width), limit_ref[0], F32)
            near = rounded(edge)
            below = jnp.where(near < edge, near, rounded(near * (1.0 - 2.0**-8)))
            above = jnp.where(near < edge, rounded(near * (1.0 + 1.5 * 2.0**-8)), near)
        for number, out in enumerate(outs):
            part = values_ref[lax.rem(place + number, seqs)]
            if limit is not None:
                size = jnp.abs(part)
                coarse = rounded(size)
                coarse = jnp.where(size < edge, jnp.minimum(coarse, below), jnp.maximum(coarse, above))
                part = jnp.where(part < 0, -coarse, coarse)
            out[...] = part.astype(BF16)

    smem_spec = pl.BlockSpec(memory_space=pltpu.SMEM)
    *parts, place = pl.pallas_call(
        kernel,
        grid=(rows // block,),
        in_specs=[smem_spec, pl.BlockSpec((seqs, block, width), lambda i: (0, i, 0))],
        out_specs=[pl.BlockSpec((block, width), lambda i: (i, 0))] * seqs + [smem_spec],
        out_shape=[jax.ShapeDtypeStruct((rows, width), BF16)] * seqs + [jax.ShapeDtypeStruct((1,), jnp.int32)],
        compiler_params=pltpu.CompilerParams(vmem_limit_bytes=56 << 20),
        cost_estimate=SHORT,
    )(jnp.zeros((1,), F32) if limit is None else limit, values)
    return parts, place[0]


def unpack(parts):
    seqs = len(parts)
    rows, width = parts[0].shape
    block = min(256, rows)

    def kernel(*refs):
        place = lax.axis_index("seq")
        for number, ref in enumerate(refs[:seqs]):
            refs[seqs][lax.rem(place + number, seqs)] = ref[...].astype(F32)

    return pl.pallas_call(
        kernel,
        grid=(rows // block,),
        in_specs=[pl.BlockSpec((block, width), lambda i: (i, 0))] * seqs,
        out_specs=pl.BlockSpec((seqs, block, width), lambda i: (0, i, 0)),
        out_shape=jax.ShapeDtypeStruct((seqs, rows, width), F32),
        compiler_params=pltpu.CompilerParams(vmem_limit_bytes=56 << 20),
        cost_estimate=SHORT,
    )(*parts)


def project(limit, tokens, pieces, biases):
    rows, width = tokens[0].shape
    pairs, along, piece_rows, columns = pieces[0].shape
    block = min(512, rows)
    steps = rows // block

    def kernel(limit_ref, own_ref, other_ref, bias_ref, same_ref, across_ref, *refs):
        q_ref, kv_ref, matrix_ref, bound_ref, held, lengths, sems = refs
        step = pl.program_id(0)
        core, seq = lax.axis_index("core"), lax.axis_index("seq")
        matrix = held.reshape(width, columns)
        store = pltpu.make_async_copy(matrix, matrix_ref, sems.at[2 * pairs * along])

        @pl.when(step == 0)
        def _():
            loads = []
            for far in range(pairs):
                for number, (piece, half) in enumerate(((same_ref, core), (across_ref, 1 - core))):
                    for near in range(along):
                        place = held.at[far, half, seq ^ near]
                        sem = sems.at[(2 * far + number) * along + near]
                        loads.append(pltpu.make_async_copy(piece.at[far, near], place, sem))
            for copy in loads:
                copy.start()
            for copy in loads:
                copy.wait()
            slots = [slice(256 * number, 256 * (number + 1)) for number in range(width // 256)]
            for number in range(3):
                lanes = slice(width * number, width * (number + 1))
                largest = jnp.zeros((256, width), F32)
                for slot in slots:
                    largest = jnp.maximum(largest, jnp.abs(matrix[slot, lanes].astype(F32)))
                top = jnp.full((1, width), 0.5 * jnp.max(largest), F32).astype(BF16)
                for slot in slots:
                    matrix[slot, lanes] = jnp.maximum(jnp.minimum(matrix[slot, lanes], top), -top)
            store.start()
            lengths[...] = jnp.zeros_like(lengths)

        top = jnp.full((1, width), limit_ref[0], F32).astype(BF16)

        def clipped(ref):
            return jnp.maximum(jnp.minimum(ref[...], top), -top)

        @pl.when(step < steps)
        def _():
            all_three = dots(clipped(own_ref), matrix[...], NN) + bias_ref[...]
            q = all_three[:, :width].astype(BF16) * jnp.asarray(HD**-0.5, BF16)
            q_ref[...] = q
            kv_ref[...] = all_three[:, width:].astype(BF16)
            lengths[0:1] = jnp.maximum(lengths[0:1], head_lengths(q))

        @pl.when(step >= steps)
        def _():
            kv_ref[...] = (dots(clipped(other_ref), matrix[:, width:], NN) + bias_ref[:, width:]).astype(BF16)

        lengths[1:2] = jnp.maximum(lengths[1:2], head_lengths(kv_ref[:, :width]))

        @pl.when(step == 2 * steps - 1)
        def _():
            bound_ref[0] = jnp.max(lengths[0:1] * lengths[1:2])
            store.wait()

    any_spec = pl.BlockSpec(memory_space=pl.ANY)
    smem_spec = pl.BlockSpec(memory_space=pltpu.SMEM)
    return pl.pallas_call(
        kernel,
        grid=(2 * steps,),
        in_specs=[
            smem_spec,
            pl.BlockSpec((block, width), lambda i: (jnp.minimum(i, steps - 1), 0)),
            pl.BlockSpec((block, width), lambda i: (jnp.maximum(i - steps, 0), 0)),
            pl.BlockSpec((1, columns), lambda i: (0, 0)),
            any_spec,
            any_spec,
        ],
        out_specs=[
            pl.BlockSpec((block, width), lambda i: (jnp.minimum(i, steps - 1), 0)),
            pl.BlockSpec((block, 2 * width), lambda i: (i, 0)),
            any_spec,
            smem_spec,
        ],
        out_shape=[
            jax.ShapeDtypeStruct((rows, width), BF16),
            jax.ShapeDtypeStruct((2 * rows, 2 * width), BF16),
            jax.ShapeDtypeStruct((width, columns), BF16),
            jax.ShapeDtypeStruct((1,), F32),
        ],
        scratch_shapes=[
            pltpu.VMEM((pairs, 2, along, piece_rows, columns), BF16),
            pltpu.VMEM((8, LANES), F32),
            pltpu.SemaphoreType.DMA((2 * pairs * along + 1,)),
        ],
        compiler_params=pltpu.CompilerParams(vmem_limit_bytes=56 << 20),
        cost_estimate=SHORT,
    )(limit, tokens[0], tokens[1], biases, *pieces)


def attend(bound, queries, keys_values, start, count, filled=None):
    seqs, rows, width = queries.shape
    keys = keys_values.shape[1]
    pairs = width // LANES
    block = min(256, rows)
    held = [] if filled is None else list(filled)

    def kernel(bound_ref, q_ref, k_ref, v_ref, *refs):
        o_ref, l_ref, p_ref, token_ref = refs[len(held) :]
        low = lax.broadcasted_iota(jnp.int32, (1, LANES), 1) < HD
        q = q_ref[0]
        token_ref[...] = jnp.zeros_like(token_ref)

        def fill(shifted):
            outs, inverses = [], []
            for half in range(2):
                mine = low if half == 0 else ~low
                scores = dots(jnp.where(mine, q, jnp.zeros_like(q)), k_ref[0], NT)
                if shifted:
                    scores = scores - jnp.max(scores, axis=-1, keepdims=True)
                weights = jnp.exp(scores)
                inverse = 1.0 / jnp.sum(weights, axis=-1, keepdims=True)
                weights = weights.astype(BF16)
                p_ref[0, half] = weights
                outs.append(dots(weights, v_ref[0], NN) * inverse)
                inverses.append(inverse)
            o_ref[0] = jnp.where(low, outs[0], outs[1]).astype(BF16)
            l_ref[0] = jnp.where(low, inverses[0], inverses[1])

        small = bound_ref[0] < SAFE_SCORE**2

        @pl.when(small)
        def _():
            fill(False)

        @pl.when(jnp.logical_not(small))
        def _():
            fill(True)

    rows_spec = pl.BlockSpec((1, block, LANES), lambda s, p, i: (s, i, start + p))
    return pl.pallas_call(
        kernel,
        grid=(seqs, count, rows // block),
        in_specs=[
            pl.BlockSpec(memory_space=pltpu.SMEM),
            rows_spec,
            pl.BlockSpec((1, keys, LANES), lambda s, p, i: (s, 0, start + p)),
            pl.BlockSpec((1, keys, LANES), lambda s, p, i: (s, 0, pairs + start + p)),
        ]
        + [pl.BlockSpec(memory_space=pl.ANY)] * len(held),
        out_specs=[
            rows_spec,
            rows_spec,
            pl.BlockSpec((1, 2, block, keys), lambda s, p, i: (s, start + p, i, 0)),
            pl.BlockSpec((8, LANES), lambda s, p, i: (0, 0)),
        ],
        out_shape=[
            jax.ShapeDtypeStruct((seqs, rows, width), BF16),
            jax.ShapeDtypeStruct((seqs, rows, width), F32),
            jax.ShapeDtypeStruct((seqs, 2 * pairs, rows, keys), BF16),
            jax.ShapeDtypeStruct((8, LANES), F32),
        ],
        input_output_aliases={4 + i: i for i in range(len(held))},
        compiler_params=pltpu.CompilerParams(vmem_limit_bytes=56 << 20),
        cost_estimate=SHORT,
    )(bound, queries, keys_values, keys_values, *held)


def attend_back(queries, keys_values, context, inverse, context_grad, weights, start, count, filled=None):
    seqs, rows, width = queries.shape
    keys = keys_values.shape[1]
    pairs = width // LANES
    block = min(512, rows)
    held = [] if filled is None else list(filled)

    def kernel(q_ref, k_ref, v_ref, o_ref, l_ref, do_ref, p_ref, *refs):
        dq_ref, dk_ref, dv_ref, sums_ref, token_ref, dk_sum, dv_sum = refs[len(held) :]
        step = pl.program_id(2)
        low = lax.broadcasted_iota(jnp.int32, (1, LANES), 1) < HD
        q, do = q_ref[0], (do_ref[0].astype(F32) * l_ref[0]).astype(BF16)
        product = do.astype(F32) * o_ref[0].astype(F32)
        q_turned, do_turned = q.T, do.T

        @pl.when(step == 0)
        def _():
            dk_sum[...] = jnp.zeros_like(dk_sum)
            dv_sum[...] = jnp.zeros_like(dv_sum)
            sums_ref[...] = jnp.zeros_like(sums_ref)
            token_ref[...] = jnp.zeros_like(token_ref)

        grads = []
        for half in range(2):
            mine = low if half == 0 else ~low
            lanes = slice(half * HD, (half + 1) * HD)
            delta = jnp.sum(jnp.where(mine, product, 0.0), axis=-1, keepdims=True)
            raised = dots(jnp.where(mine, do, jnp.zeros_like(do)), v_ref[0], NT)
            p = p_ref[0, half]
            ds = (raised - delta).astype(BF16) * p
            grads.append(dots(ds, k_ref[0], NN))
            dk_sum[lanes] += dots(q_turned[lanes], ds, NN)
            dv_sum[lanes] += dots(do_turned[lanes], p, NN)
        dq = (jnp.where(low, grads[0], grads[1]) * HD**-0.5).astype(BF16)
        dq_ref[0] = dq
        sums_ref[0, 0:1] += jnp.sum(dq.astype(F32), axis=0, keepdims=True)

        @pl.when(step == pl.num_programs(2) - 1)
        def _():
            dk_ref[0] = dk_sum[...].T.astype(BF16)
            dv = dv_sum[...].T.astype(BF16)
            dv_ref[0] = dv
            sums_ref[0, 1:2] = jnp.sum(dv.astype(F32), axis=0, keepdims=True)

    rows_spec = pl.BlockSpec((1, block, LANES), lambda s, p, i: (s, i, start + p))
    keys_spec = pl.BlockSpec((1, keys, LANES), lambda s, p, i: (s, 0, start + p))
    return pl.pallas_call(
        kernel,
        grid=(seqs, count, rows // block),
        in_specs=[
            rows_spec,
            keys_spec,
            pl.BlockSpec((1, keys, LANES), lambda s, p, i: (s, 0, pairs + start + p)),
            rows_spec,
            rows_spec,
            rows_spec,
            pl.BlockSpec((1, 2, block, keys), lambda s, p, i: (s, start + p, i, 0)),
        ]
        + [pl.BlockSpec(memory_space=pl.ANY)] * len(held),
        out_specs=[
            rows_spec,
            keys_spec,
            keys_spec,
            pl.BlockSpec((1, 8, LANES), lambda s, p, i: (s, 0, start + p)),
            pl.BlockSpec((8, LANES), lambda s, p, i: (0, 0)),
        ],
        out_shape=[
            jax.ShapeDtypeStruct((seqs, rows, width), BF16),
            jax.ShapeDtypeStruct((seqs, keys, width), BF16),
            jax.ShapeDtypeStruct((seqs, keys, width), BF16),
            jax.ShapeDtypeStruct((seqs, 8, width), F32),
            jax.ShapeDtypeStruct((8, LANES), F32),
        ],
        input_output_aliases={7 + i: i for i in range(len(held))},
        scratch_shapes=[pltpu.VMEM((LANES, keys), F32), pltpu.VMEM((LANES, keys), F32)],
        compiler_params=pltpu.CompilerParams(vmem_limit_bytes=56 << 20),
        cost_estimate=SHORT,
    )(queries, keys_values, keys_values, context, inverse, context_grad, weights, *held)


def back_to_tokens(terms, matrix, first_row, rows, finish=None, pieces=1):
    width, columns = matrix.shape
    block = rows // pieces if pieces > 1 else min(512, rows)
    shift = first_row // block
    extra = [] if finish is None else list(finish)

    def kernel(*refs):
        matrix_ref, parts, refs = refs[0], refs[1 : 1 + len(terms)], refs[1 + len(terms) :]
        total = None
        for ref, (part, column) in zip(parts, terms):
            product = dots(ref[...], matrix_ref[:, column : column + part.shape[1]], NT)
            total = product if total is None else total + product
        if finish is not None:
            limit_ref, arrived_ref, zero_ref, tokens_ref, *outs = refs
            total = total + arrived_ref[...].astype(F32)
            inside = jnp.abs(tokens_ref[...].astype(F32)) < limit_ref[0]
            total = zero_ref[...].astype(F32) + jnp.where(inside, total, 0.0)
        else:
            outs = refs
        if pieces == 1:
            outs[0][...] = total.astype(BF16)
        for number, out in enumerate(outs if pieces > 1 else []):

            @pl.when(pl.program_id(0) == number)
            def _(out=out):
                out[...] = total.astype(BF16)

    row_spec = pl.BlockSpec((block, width), lambda i: (i, 0))
    return pl.pallas_call(
        kernel,
        grid=(rows // block,),
        in_specs=[pl.BlockSpec((width, columns), lambda i: (0, 0), pipeline_mode=pl.Buffered(1))]
        + [pl.BlockSpec((block, part.shape[1]), lambda i: (shift + i, 0)) for part, _ in terms]
        + ([] if finish is None else [pl.BlockSpec(memory_space=pltpu.SMEM)] + [row_spec] * 3),
        out_specs=row_spec if pieces == 1 else [pl.BlockSpec((block, width), lambda i: (0, 0))] * pieces,
        out_shape=(
            jax.ShapeDtypeStruct((rows, width), BF16)
            if pieces == 1
            else [jax.ShapeDtypeStruct((block, width), BF16)] * pieces
        ),
        compiler_params=pltpu.CompilerParams(vmem_limit_bytes=56 << 20),
        cost_estimate=SHORT,
    )(matrix, *[part for part, _ in terms], *extra)


def weight_grads(limit, tokens, chunks, sums, shape):
    rows, width = tokens[0].shape
    block = min(512, rows)
    steps = rows // block
    spans = [chunk[0].shape[1] for chunk in chunks]
    columns = 3 * width + LANES
    pairs, along = shape
    piece_rows = width // (2 * pairs * along)

    def kernel(limit_ref, own_ref, other_ref, sums_ref, *refs):
        grads, (mine_ref, theirs_ref, total, held, sems) = refs[: 3 * len(chunks)], refs[3 * len(chunks) :]
        step = pl.program_id(0)
        core = lax.axis_index("core")
        top = jnp.full((1, width), limit_ref[0], F32).astype(BF16)

        @pl.when(step == 0)
        def _():
            total[...] = jnp.zeros_like(total)

        def add(tokens_ref, kinds):
            turned = jnp.maximum(jnp.minimum(tokens_ref[...], top), -top).T
            for number, span in enumerate(spans):
                for kind in kinds:
                    start = width * kind + sum(spans[:number])
                    total[:, start : start + span] += dots(turned, grads[3 * number + kind][...], NN)

        @pl.when(step < steps)
        def _():
            add(own_ref, (0, 1, 2))

        @pl.when(step >= steps)
        def _():
            add(other_ref, (1, 2))

        @pl.when(step == 2 * steps - 1)
        def _():
            part = held.shape[:-1]
            held[..., : 3 * width] = total[...].astype(BF16).reshape(part + (3 * width,))
            rows_of = jnp.concatenate([sums_ref[...], jnp.zeros((LANES - sums_ref.shape[0], width), F32)], axis=0)
            held[..., 3 * width :] = rows_of.T.astype(BF16).reshape(part + (LANES,))
            stores = []
            for far in range(pairs):
                for number, (target, half) in enumerate(((mine_ref, core), (theirs_ref, 1 - core))):
                    stores.append(pltpu.make_async_copy(held.at[far, half], target.at[far], sems.at[2 * far + number]))
            for copy in stores:
                copy.start()
            for copy in stores:
                copy.wait()

    smem_spec = pl.BlockSpec(memory_space=pltpu.SMEM)

    def specs(span):
        own_spec = pl.BlockSpec((block, span), lambda i: (jnp.minimum(i, steps - 1), 0))
        return [own_spec] + [pl.BlockSpec((block, span), lambda i: (i, 0))] * 2

    part = jax.ShapeDtypeStruct((pairs, along, piece_rows, columns), BF16)
    return pl.pallas_call(
        kernel,
        grid=(2 * steps,),
        in_specs=[
            smem_spec,
            pl.BlockSpec((block, width), lambda i: (jnp.minimum(i, steps - 1), 0)),
            pl.BlockSpec((block, width), lambda i: (jnp.maximum(i - steps, 0), 0)),
            pl.BlockSpec(sums.shape, lambda i: (0, 0)),
        ]
        + [spec for span in spans for spec in specs(span)],
        out_specs=[pl.BlockSpec(memory_space=pl.ANY)] * 2,
        out_shape=[part, part],
        scratch_shapes=[
            pltpu.VMEM((width, 3 * width), F32),
            pltpu.VMEM((pairs, 2, along, piece_rows, columns), BF16),
            pltpu.SemaphoreType.DMA((2 * pairs,)),
        ],
        compiler_params=pltpu.CompilerParams(vmem_limit_bytes=56 << 20),
        cost_estimate=SHORT,
    )(limit, tokens[0], tokens[1], sums, *[grad for chunk in chunks for grad in chunk])


def middle(context, residual, cotangent, weights, vectors, up_bias, shape):
    rows, width = residual.shape
    units = up_bias.shape[1]
    pairs, along = shape
    block = min(512, rows)
    blocks = units // width
    parts = len(weights)
    whole = parts == 2
    share = width // (2 * pairs * along)
    if whole:
        first_shape = (pairs, 2, along * share, width + units)
        second_shape = (pairs, 2, along * share * blocks, width)
    else:
        first_shape = (pairs, 2, along, share, width + units)
        second_shape = (pairs, 2, along, blocks, share, width)
    copies = 2 if whole else 2 * pairs * (1 + blocks)

    def kernel(residual_ref, cot_ref, vector_ref, bias_ref, *refs):
        context_ref, refs = refs[0], refs[1:]
        weight_refs, refs = refs[:parts], refs[parts:]
        result_ref, zero_ref, back_ref, packed_ref, *outs, small_ref, small_up_ref, first, second, grad_output, grad_up, grad_down = refs[:-3]
        act_ref, slope_ref, sems = refs[-3:]
        step = pl.program_id(0)
        pair, core = lax.axis_index("pair"), lax.axis_index("core")

        def matches(pieces):
            if whole:
                return [(pieces[0], first), (pieces[1], second)]
            found = []
            for piece, place, half in pieces:
                found.append((piece.at[:, :, : width + units], first.at[place, half]))
                for j in range(blocks):
                    lanes = slice(width + units + width * j, width + units + width * (j + 1))
                    found.append((piece.at[:, :, lanes], second.at[place, half].at[:, j]))
            return found

        halves = core, 1 - core
        if whole:
            sources, targets = weight_refs, outs
        else:
            sources = [(ref, pair ^ (i // 2), halves[i % 2]) for i, ref in enumerate(weight_refs)]
            targets = [(out.at[far], pair ^ far, half) for far in range(pairs) for out, half in zip(outs, halves)]
        loads = [
            pltpu.make_async_copy(outside, place, sems.at[i]) for i, (outside, place) in enumerate(matches(sources))
        ]

        @pl.when(step == 0)
        def _():
            for copy in loads:
                copy.start()
            small_ref[...] = jnp.zeros_like(small_ref)
            small_up_ref[...] = jnp.zeros_like(small_up_ref)
            grad_output[...] = jnp.zeros_like(grad_output)
            grad_up[...] = jnp.zeros_like(grad_up)
            grad_down[...] = jnp.zeros_like(grad_down)
            for copy in loads:
                copy.wait()

        def vector(number):
            return vector_ref[number : number + 1]

        def mean(values):
            return jnp.mean(values, axis=-1, keepdims=True)

        def columns(j):
            return slice(width * j, width * (j + 1))

        def output_matrix():
            return first[(..., slice(0, width))].reshape(width, width)

        def up_matrix(j):
            return first[(..., slice(width * (j + 1), width * (j + 2)))].reshape(width, width)

        down_rows = second.reshape(units, width)

        bias_output, bias_down, gain_one, shift_one, gain_two, shift_two = [vector(i) for i in range(6)]
        ctx = context_ref[...]
        zero = residual_ref[...].astype(F32) + dots(ctx, output_matrix(), NN) + bias_output
        center = zero - mean(zero)
        scale_one = lax.rsqrt(mean(center * center) + NORM_EPS)
        normal_one = center * scale_one
        hidden = normal_one * gain_one + shift_one
        hidden_low = hidden.astype(BF16)
        summed = hidden + bias_down
        for j in range(blocks):
            up = dots(hidden_low, up_matrix(j), NN) + bias_ref[:, columns(j)]
            below = 0.5 + 0.5 * lax.erf(up * 0.7071067811865476)
            act = (up * below).astype(BF16)
            act_ref[:, columns(j)] = act
            slope = below + up * (0.3989422804014327 * jnp.exp(-0.5 * up * up))
            slope_ref[:, columns(j)] = slope.astype(BF16)
            summed = summed + dots(act, down_rows[columns(j)], NN)
        center = summed - mean(summed)
        scale_two = lax.rsqrt(mean(center * center) + NORM_EPS)
        normal_two = center * scale_two
        result_ref[...] = (normal_two * gain_two + shift_two).astype(result_ref.dtype)

        cot = cot_ref[...].astype(F32)
        scaled = cot * gain_two
        grad_summed = scale_two * (scaled - mean(scaled) - normal_two * mean(scaled * normal_two))
        down_low = grad_summed.astype(BF16)
        grad_hidden = grad_summed
        for j in range(blocks):
            lifted = dots(down_low, down_rows[columns(j)], NT) * slope_ref[:, columns(j)].astype(F32)
            up_low = lifted.astype(BF16)
            small_up_ref[:, columns(j)] += jnp.sum(up_low.astype(F32), axis=0, keepdims=True)
            grad_up[:, columns(j)] += dots(hidden_low, up_low, TN)
            grad_hidden = grad_hidden + dots(up_low, up_matrix(j), NT)
            grad_down[columns(j)] += dots(act_ref[:, columns(j)], down_low, TN)
        scaled = grad_hidden * gain_one
        grad_zero = scale_one * (scaled - mean(scaled) - normal_one * mean(scaled * normal_one))
        branch_low = grad_zero.astype(BF16)
        zero_ref[...] = branch_low
        grad_output[...] += dots(ctx, branch_low, TN)
        back_ref[...] = dots(branch_low, output_matrix(), NT).astype(BF16)
        sums = [branch_low.astype(F32), down_low.astype(F32), grad_hidden * normal_one, grad_hidden, cot * normal_two, cot]
        for number, terms in enumerate(sums):
            small_ref[number : number + 1] += jnp.sum(terms, axis=0, keepdims=True)

        @pl.when(step == pl.num_programs(0) - 1)
        def _():
            part = first.shape[:-1] + (width,)
            first[(..., slice(0, width))] = grad_output[...].astype(BF16).reshape(part)
            for j in range(blocks):
                lanes = slice(width * (j + 1), width * (j + 2))
                first[(..., lanes)] = grad_up[:, columns(j)].astype(BF16).reshape(part)
            second[...] = grad_down[...].astype(BF16).reshape(second.shape)
            stores = [
                pltpu.make_async_copy(place, outside, sems.at[i]) for i, (outside, place) in enumerate(matches(targets))
            ]
            for copy in stores:
                copy.start()
            packed_ref[...] = jnp.zeros_like(packed_ref)
            for device in range(2 * pairs * along):
                packed_ref[device, :8, :share] = small_ref[:, share * device : share * (device + 1)]
                up_lanes = slice(share * blocks * device, share * blocks * (device + 1))
                packed_ref[device, 8:9, : share * blocks] = small_up_ref[:, up_lanes]
            for copy in stores:
                copy.wait()

    any_spec = pl.BlockSpec(memory_space=pl.ANY)
    row_spec = pl.BlockSpec((block, width), lambda i: (i, 0))
    if whole:
        grads = [jax.ShapeDtypeStruct(first_shape, BF16), jax.ShapeDtypeStruct(second_shape, BF16)]
    else:
        grads = [jax.ShapeDtypeStruct((pairs, along, share, width + 2 * units), BF16)] * 2
    return pl.pallas_call(
        kernel,
        grid=(rows // block,),
        in_specs=[row_spec] * 2
        + [pl.BlockSpec((8, width), lambda i: (0, 0)), pl.BlockSpec((1, units), lambda i: (0, 0))]
        + [row_spec]
        + [any_spec] * parts,
        out_specs=[row_spec] * 3
        + [pl.BlockSpec((2 * pairs * along, 16, LANES), lambda i: (0, 0, 0))]
        + [any_spec] * 2,
        out_shape=[
            jax.ShapeDtypeStruct((rows, width), BF16),
            jax.ShapeDtypeStruct((rows, width), BF16),
            jax.ShapeDtypeStruct((rows, width), BF16),
            jax.ShapeDtypeStruct((2 * pairs * along, 16, LANES), F32),
            *grads,
        ],
        scratch_shapes=[
            pltpu.VMEM((8, width), F32),
            pltpu.VMEM((1, units), F32),
            pltpu.VMEM(first_shape, BF16),
            pltpu.VMEM(second_shape, BF16),
            pltpu.VMEM((width, width), F32),
            pltpu.VMEM((width, units), F32),
            pltpu.VMEM((units, width), F32),
            pltpu.VMEM((block, units), BF16),
            pltpu.VMEM((block, units), BF16),
            pltpu.SemaphoreType.DMA((copies,)),
        ],
        compiler_params=pltpu.CompilerParams(vmem_limit_bytes=62 << 20),
        cost_estimate=SHORT,
    )(residual, cotangent, vectors, up_bias, context, *weights)


def after(values, *earlier):
    return lax.optimization_barrier((values, earlier))[0]


class Plan:
    def __init__(self, pairs, along, seqs):
        self.pairs, self.along, self.seqs = pairs, along, seqs
        self.devices = 2 * pairs * along
        self.by_chip = 2 * seqs == along and pairs == 4 and along & (along - 1) == 0

    def moves(self, number):
        table = []
        for pair in range(self.pairs):
            for core in range(2):
                for place in range(self.along):
                    source = (pair * 2 + core) * self.along + place
                    chip = core * self.seqs + (place + number) % self.seqs
                    target = (pair * 2 + 1 - place // self.seqs) * self.along + chip
                    table.append((source, target))
        return table

    def send(self, part, number, *earlier):
        return lax.ppermute(after(part, *earlier), AXES, self.moves(number))

    def send_home(self, worked):
        blocks = worked if isinstance(worked, (list, tuple)) else worked.reshape(self.seqs, -1, worked.shape[-1])
        if not self.by_chip:
            return blocks
        return [
            lax.ppermute(blocks[number], AXES, [(b, a) for a, b in self.moves(number)]) for number in range(self.seqs)
        ]

    def at_home(self, back):
        return unpack(back) if self.by_chip else back.astype(F32)

    def swap(self, values):
        return lax.ppermute(values, "core", [(0, 1), (1, 0)])

    def meet(self, values, axis, far):
        count = lax.axis_size(axis)
        return lax.ppermute(values, axis, [(i, i ^ far) for i in range(count)])

    def column(self, rows, *earlier):
        return [rows] + after([self.meet(rows, "seq", far) for far in range(1, self.along)], *earlier)

    def ordered(self, column, here):
        held = jnp.zeros((self.along,) + column[0].shape, column[0].dtype)
        for far in range(self.along):
            held = lax.dynamic_update_index_in_dim(held, column[far], here ^ far, 0)
        return held

    def both_cores(self, pieces):
        return [part for piece in pieces for part in (piece, self.swap(piece))]

    def add_cores(self, mine, theirs, *earlier):
        theirs = after(self.swap(theirs), *earlier)
        return (mine.astype(F32) + theirs.astype(F32)).astype(BF16)

    def add_blocks(self, mine, theirs, *earlier):
        theirs = after(self.swap(theirs), *earlier)
        return [(mine[far].astype(F32) + theirs[far].astype(F32)).astype(BF16) for far in range(self.pairs)]

    def spread(self, column):
        copies = jnp.broadcast_to(column[None], (self.pairs,) + column.shape)
        return lax.all_to_all(copies, "pair", split_axis=0, concat_axis=0, tiled=True)

    def near_and_far(self, column):
        return [column] + [self.meet(column, "pair", far) for far in range(1, self.pairs)]

    def total_along(self, values, *earlier):
        return self.gathered(values, "seq", *earlier)

    def gathered(self, parts, axis, *earlier):
        arrived = after([self.meet(parts[far], axis, far) for far in range(1, len(parts))], *earlier)
        total = parts[0].astype(F32)
        for part in arrived:
            total = total + part.astype(F32)
        return total

    def total(self, parts, axis):
        arrived = lax.all_to_all(parts, axis, split_axis=0, concat_axis=0, tiled=True)
        return jnp.sum(arrived.astype(F32), axis=0)

    def everywhere(self, values):
        copies = jnp.broadcast_to(values[None], (self.devices,) + values.shape)
        return lax.all_to_all(copies, AXES, split_axis=0, concat_axis=0, tiled=True)

    def exchange(self, parts):
        return lax.all_to_all(parts, AXES, split_axis=0, concat_axis=0, tiled=True)

    def gather(self, rows):
        return lax.all_gather(rows, AXES, axis=0, tiled=True)

    def scatter(self, total):
        return lax.psum_scatter(total, AXES, scatter_dimension=0, tiled=True)


def local(plan, tokens, cotangent, *rest):
    params, clip_limits = rest[:15], rest[15]
    limit = clip_limits[0]
    matrices = params[:6]
    width = tokens.shape[-1]
    units = matrices[4].shape[1]
    devices = plan.devices

    chosen, place = parcel(tokens, clip_limits)
    if plan.by_chip:
        qkv_rows, rest_rows, packed = prepare(matrices, params[6:])
        qkv_column = jnp.stack(plan.column(qkv_rows))
        vectors = plan.everywhere(packed)
        coarse = jnp.concatenate([plan.send(part, i, vectors) for i, part in enumerate(chosen)], axis=0)
        vectors = vectors.astype(F32)
        sizes = [vector.shape[0] for vector in params[6:]]
        vectors, terms = [vectors[:, i, :size].reshape(-1) for i, size in enumerate(sizes)], vectors[:, len(sizes), :18]
        limits = 0.5 * jnp.max(terms[:, :6] + terms[:, 6:12] + terms[:, 12:18], axis=0)
    else:
        coarse = jnp.roll(jnp.stack(chosen), place, axis=0).reshape(-1, width)
        vectors = [lax.all_gather(vector.astype(BF16), AXES, axis=0, tiled=True).astype(F32) for vector in params[6:]]
        limits = 0.5 * lax.pmax(jnp.stack([jnp.max(jnp.abs(matrix)) for matrix in matrices]), AXES)
    bias_query, bias_value, bias_output, bias_up, bias_down, gain_one, shift_one, gain_two, shift_two = vectors
    biases = jnp.concatenate([bias_query, jnp.zeros_like(bias_value), bias_value])[None]
    limit_low = limit.astype(BF16)

    def clip_to(number):
        return jnp.clip(matrices[number], -limits[number], limits[number]).astype(BF16)

    if plan.by_chip:
        seqs, keys = 1, 2 * coarse.shape[0]
        chosen_cotangent = parcel(after(cotangent, chosen), None)[0]
        ceilings = [jnp.full((size,), top, BF16) for size, top in zip((width, units, units), limits[3:].astype(BF16))]
        ceilings = jnp.concatenate(ceilings)[None, None]
        rest_column = plan.ordered(plan.column(after(rest_rows, qkv_column)), place)
        rest_column = jnp.clip(rest_column, -ceilings, ceilings)
        rest_pieces = plan.near_and_far(rest_column)
        qkv_same = plan.spread(qkv_column)
        qkv_across = plan.swap(qkv_same)
        coarse, chosen_cotangent = after((coarse, chosen_cotangent), rest_column, qkv_across)
        other = plan.swap(coarse)
        queries, keys_values, matrix, bound = project(clip_limits, [coarse, other], [qkv_same, qkv_across], biases)
        cotangent_low = [plan.send(chosen_cotangent[0], 0)]
        cotangent_low += [plan.send(part, i + 1, queries) for i, part in enumerate(chosen_cotangent[1:])]
    else:
        seqs = tokens.shape[0]
        every = lax.all_gather(coarse.reshape(tokens.shape), "seq", axis=1, tiled=True)
        keys = every.shape[1]
        every = every.reshape(-1, width)
        matrix = plan.gather(jnp.concatenate([matrix.astype(BF16) for matrix in matrices[:3]], axis=1))
        ceilings = jnp.repeat(limits[:3].astype(BF16), width)[None]
        matrix = jnp.clip(matrix, -ceilings, ceilings)
        all_keys = jnp.clip(every, -limit_low, limit_low)
        clipped = jnp.clip(coarse, -limit_low, limit_low)
        queries = dots(clipped, matrix[:, :width], NN) + biases[:, :width]
        queries = queries.astype(BF16) * jnp.asarray(HD**-0.5, BF16)
        keys_values = (dots(all_keys, matrix[:, width:], NN) + biases[:, width:]).astype(BF16)
        lengths = [
            jnp.sum(jnp.square(part.astype(F32)).reshape(-1, width // HD, HD), axis=-1).max(axis=0)
            for part in (queries, keys_values[:, :width])
        ]
        bound = jnp.max(lengths[0] * lengths[1])[None]
        cotangent_low = cotangent.astype(BF16).reshape(-1, width)
        rest_weights = [
            plan.gather(jnp.concatenate([clip_to(3), clip_to(4)], axis=1)).reshape(plan.pairs, 2, -1, width + units),
            plan.gather(clip_to(5)).reshape(plan.pairs, 2, -1, width),
        ]
    rows = coarse.shape[0] // seqs

    queries = queries.reshape(seqs, rows, width)
    keys_values = keys_values.reshape(seqs, keys, 2 * width)
    filled = None
    for number, count in enumerate(GROUPS):
        *filled, token = attend(bound, queries, keys_values, sum(GROUPS[:number]), count, filled)
        queries, keys_values = after((queries, keys_values), token)
    if plan.by_chip:
        cotangent_low = jnp.concatenate(cotangent_low, axis=0)
        rest_pieces = after(rest_pieces, token, cotangent_low)
        rest_weights = plan.both_cores(rest_pieces)
    context, inverse, weights = filled
    six = [bias_output, bias_down, gain_one, shift_one, gain_two, shift_two]
    six = jnp.stack(six + [jnp.zeros_like(bias_down)] * 2)
    result, grad_zero, context_grad, small, *grads = middle(
        context.reshape(-1, width),
        coarse,
        cotangent_low,
        rest_weights,
        six,
        bias_up[None],
        (plan.pairs, plan.along),
    )
    layer_out = result if plan.by_chip else plan.send_home(result)
    mids = grads
    small = plan.exchange(small)

    context_grad = context_grad.reshape(seqs, rows, width)
    filled = None
    for number, count in enumerate(BACK_GROUPS):
        *filled, token = attend_back(
            queries, keys_values, context, inverse, context_grad, weights, sum(BACK_GROUPS[:number]), count, filled
        )
        if plan.by_chip and number == 0:
            low = plan.add_blocks(mids[0], mids[1], token)
            context_grad, low = after((context_grad, low))
            rest_sum = plan.gathered(low, "pair").astype(BF16)
            layer_out = plan.send_home(after(result, token))
        context_grad = after(context_grad, token)
    grads = [grad.reshape(-1, width) for grad in filled[:3]]
    sums = jnp.sum(filled[3], axis=0)
    key_terms = [(grads[1], width), (grads[2], 2 * width)]
    local_rows = coarse.shape[0]
    if plan.by_chip:
        leaving = back_to_tokens(key_terms, matrix, local_rows, local_rows)
        arrived = plan.swap(leaving)
        layer_out, rest_sum, small, grads = after((layer_out, rest_sum, small, grads), leaving)
        rest_sum = [
            lax.dynamic_index_in_dim(rest_sum, place ^ far, 0, keepdims=False) for far in range(plan.along)
        ]
        rest_sum, sums = after((rest_sum, sums))
        mine, theirs = weight_grads(clip_limits, [coarse, other], [grads], sums, (plan.pairs, plan.along))
        arrived = after(arrived, mine)
        late = plan.add_cores(mine, theirs)
        own_terms = [(grads[0], 0)] + key_terms
    else:
        partial = back_to_tokens(key_terms, matrix, 0, seqs * keys).reshape(seqs, keys, width)
        arrived = lax.psum_scatter(partial, "seq", scatter_dimension=1, tiled=True).reshape(-1, width)
        own_terms = [(grads[0], 0)]
    tokens_grad = back_to_tokens(
        own_terms, matrix, 0, local_rows, (clip_limits, arrived, grad_zero, coarse), plan.seqs if plan.by_chip else 1
    )
    if plan.by_chip:
        rest_parts = after([plan.meet(rest_sum[far], "seq", far) for far in range(1, plan.along)], tokens_grad)
        tokens_grad, rest_parts = after((tokens_grad, rest_parts))
        late = plan.total(late, "pair").astype(BF16)
        rest_grad = rest_sum[0].astype(F32)
        for part in rest_parts:
            rest_grad = rest_grad + part.astype(F32)
        late = plan.total(late, "seq")
        layer_out = after(layer_out, tokens_grad)
        bias_grads = [late[:, 3 * width + i] for i in range(2)]
        first_grad, second_grad = rest_grad[:, : width + units], rest_grad[:, width + units :]
        second_grad = jnp.concatenate(jnp.split(second_grad, units // width, axis=1), axis=0)
    else:
        late = [
            dots(left, grads[kind], TN) for kind, left in enumerate((clipped, all_keys, all_keys))
        ]
        late = plan.scatter(jnp.concatenate(late, axis=1))
        bias_grads = [plan.scatter(sums[i]) for i in range(2)]
        first_grad = plan.scatter(mids[0].reshape(width, -1)).astype(F32)
        second_grad = plan.scatter(mids[1].reshape(units, -1)).astype(F32)
    tokens_grad = plan.at_home(plan.send_home(tokens_grad))
    small = jnp.sum(after(small, tokens_grad), axis=0)
    small_up = small[8, : units // devices]
    share = width // devices
    small = [small[i, :share] for i in range(6)]
    small = [*bias_grads, small[0], small_up, *small[1:]]

    shares = [late[:, :width], late[:, width : 2 * width], late[:, 2 * width : 3 * width]]
    shares += [first_grad[:, :width], first_grad[:, width:], second_grad]
    masked = [
        jnp.where(jnp.abs(matrices[number]) < limits[number], shares[number], 0.0) for number in range(6)
    ]
    return (
        plan.at_home(layer_out),
        tokens_grad,
        *masked,
        *small,
    )


def solution(mesh):
    pairs, along = mesh.shape["batch"] // 2, mesh.shape["seq"]
    fine_mesh = Mesh(mesh.devices.reshape(pairs, 2, along), AXES)
    rows = P(("pair", "core"), "seq", None)
    matrix = P(AXES, None)
    vector = P(AXES)

    def whole(tokens, *rest):
        plan = Plan(pairs, along, tokens.shape[0] // (2 * pairs))

        def run(*args):
            return local(plan, *args)

        return jax.shard_map(
            run,
            mesh=fine_mesh,
            in_specs=(rows, rows) + (matrix,) * 6 + (vector,) * 9 + (P(),),
            out_specs=(rows, rows) + (matrix,) * 6 + (vector,) * 9,
            check_vma=False,
        )(tokens, *rest)

    return whole
```

```python
import jax
import jax.numpy as jnp
from jax import lax
from jax.experimental import pallas as pl
from jax.experimental.pallas import tpu as pltpu
from jax.sharding import Mesh, PartitionSpec as P

HD = 64
LANES = 128
NORM_EPS = 1e-12
SAFE_SCORE = 60.0
AXES = ("pair", "core", "seq")
GROUPS = (6,)
BACK_GROUPS = (1, 5)
SHORT = pl.CostEstimate(flops=1, transcendentals=0, bytes_accessed=1)
F32 = jnp.float32
BF16 = jnp.bfloat16

NT = (((1,), (1,)), ((), ()))
NN = (((1,), (0,)), ((), ()))
TN = (((0,), (0,)), ((), ()))


def dots(left, right, dims):
    return lax.dot_general(left, right, dims, preferred_element_type=F32)


def rounded(values):
    return lax.reduce_precision(values, 8, 7)


def prepare(matrices, vectors):
    rows, width = matrices[0].shape
    units = matrices[4].shape[1]
    count, number_of = len(matrices), len(vectors)

    def kernel(*refs):
        matrix_refs, vector_refs = refs[:count], refs[count : count + number_of]
        front_ref, rest_ref, packed_ref = refs[count + number_of :]
        for number in range(3):
            front_ref[:, width * number : width * (number + 1)] = matrix_refs[number][...].astype(BF16)
        rest_ref[:, :width] = matrix_refs[3][...].astype(BF16)
        rest_ref[:, width : width + units] = matrix_refs[4][...].astype(BF16)
        for j in range(units // width):
            part = matrix_refs[5][rows * j : rows * (j + 1)]
            rest_ref[:, width + units + width * j : width + units + width * (j + 1)] = part.astype(BF16)
        packed_ref[...] = jnp.zeros_like(packed_ref)
        for number, ref in enumerate(vector_refs):
            packed_ref[number : number + 1, : ref.shape[1]] = ref[...].astype(BF16)
        lane = lax.broadcasted_iota(jnp.int32, (1, LANES), 1)
        row = jnp.zeros((1, LANES), F32)
        for number, ref in enumerate(matrix_refs):
            largest = jnp.full((1, LANES), jnp.max(jnp.abs(ref[...])), F32)
            high = rounded(largest)
            middle_term = rounded(largest - high)
            for i, term in enumerate((high, middle_term, largest - high - middle_term)):
                row = jnp.where(lane == count * i + number, term, row)
        packed_ref[number_of : number_of + 1] = row.astype(BF16)

    return pl.pallas_call(
        kernel,
        out_shape=[
            jax.ShapeDtypeStruct((rows, 3 * width), BF16),
            jax.ShapeDtypeStruct((rows, width + 2 * units), BF16),
            jax.ShapeDtypeStruct((16, LANES), BF16),
        ],
        compiler_params=pltpu.CompilerParams(vmem_limit_bytes=56 << 20),
        cost_estimate=SHORT,
    )(*matrices, *[vector[None] for vector in vectors])


def head_lengths(rows):
    width = rows.shape[1]
    feature = lax.broadcasted_iota(jnp.int32, (width, LANES), 0)
    head = lax.broadcasted_iota(jnp.int32, (width, LANES), 1)
    members = jnp.where((feature >= head * HD) & (feature < (head + 1) * HD), 1.0, 0.0).astype(BF16)
    wide = rows.astype(F32)
    return jnp.max(dots((wide * wide).astype(BF16), members, NN), axis=0, keepdims=True)


def parcel(values, limit):
    seqs, rows, width = values.shape
    block = min(256, rows)

    def kernel(limit_ref, values_ref, *refs):
        outs, place_ref = refs[:seqs], refs[seqs]
        place = lax.axis_index("seq")
        place_ref[0] = place
        if limit is not None:
            edge = jnp.full((1, width), limit_ref[0], F32)
            near = rounded(edge)
            below = jnp.where(near < edge, near, rounded(near * (1.0 - 2.0**-8)))
            above = jnp.where(near < edge, rounded(near * (1.0 + 1.5 * 2.0**-8)), near)
        for number, out in enumerate(outs):
            part = values_ref[lax.rem(place + number, seqs)]
            if limit is not None:
                size = jnp.abs(part)
                coarse = rounded(size)
                coarse = jnp.where(size < edge, jnp.minimum(coarse, below), jnp.maximum(coarse, above))
                part = jnp.where(part < 0, -coarse, coarse)
            out[...] = part.astype(BF16)

    smem_spec = pl.BlockSpec(memory_space=pltpu.SMEM)
    *parts, place = pl.pallas_call(
        kernel,
        grid=(rows // block,),
        in_specs=[smem_spec, pl.BlockSpec((seqs, block, width), lambda i: (0, i, 0))],
        out_specs=[pl.BlockSpec((block, width), lambda i: (i, 0))] * seqs + [smem_spec],
        out_shape=[jax.ShapeDtypeStruct((rows, width), BF16)] * seqs + [jax.ShapeDtypeStruct((1,), jnp.int32)],
        compiler_params=pltpu.CompilerParams(vmem_limit_bytes=56 << 20),
        cost_estimate=SHORT,
    )(jnp.zeros((1,), F32) if limit is None else limit, values)
    return parts, place[0]


def unpack(parts):
    seqs = len(parts)
    rows, width = parts[0].shape
    block = min(256, rows)

    def kernel(*refs):
        place = lax.axis_index("seq")
        for number, ref in enumerate(refs[:seqs]):
            refs[seqs][lax.rem(place + number, seqs)] = ref[...].astype(F32)

    return pl.pallas_call(
        kernel,
        grid=(rows // block,),
        in_specs=[pl.BlockSpec((block, width), lambda i: (i, 0))] * seqs,
        out_specs=pl.BlockSpec((seqs, block, width), lambda i: (0, i, 0)),
        out_shape=jax.ShapeDtypeStruct((seqs, rows, width), F32),
        compiler_params=pltpu.CompilerParams(vmem_limit_bytes=56 << 20),
        cost_estimate=SHORT,
    )(*parts)


def project(limit, tokens, pieces, biases):
    rows, width = tokens[0].shape
    pairs, along, piece_rows, columns = pieces[0].shape
    block = min(512, rows)
    steps = rows // block

    def kernel(limit_ref, own_ref, other_ref, bias_ref, same_ref, across_ref, *refs):
        q_ref, kv_ref, matrix_ref, bound_ref, held, lengths, sems = refs
        step = pl.program_id(0)
        core, seq = lax.axis_index("core"), lax.axis_index("seq")
        matrix = held.reshape(width, columns)
        store = pltpu.make_async_copy(matrix, matrix_ref, sems.at[2 * pairs * along])

        @pl.when(step == 0)
        def _():
            loads = []
            for far in range(pairs):
                for number, (piece, half) in enumerate(((same_ref, core), (across_ref, 1 - core))):
                    for near in range(along):
                        place = held.at[far, half, seq ^ near]
                        sem = sems.at[(2 * far + number) * along + near]
                        loads.append(pltpu.make_async_copy(piece.at[far, near], place, sem))
            for copy in loads:
                copy.start()
            for copy in loads:
                copy.wait()
            slots = [slice(256 * number, 256 * (number + 1)) for number in range(width // 256)]
            for number in range(3):
                lanes = slice(width * number, width * (number + 1))
                largest = jnp.zeros((256, width), F32)
                for slot in slots:
                    largest = jnp.maximum(largest, jnp.abs(matrix[slot, lanes].astype(F32)))
                top = jnp.full((1, width), 0.5 * jnp.max(largest), F32).astype(BF16)
                for slot in slots:
                    matrix[slot, lanes] = jnp.maximum(jnp.minimum(matrix[slot, lanes], top), -top)
            store.start()
            lengths[...] = jnp.zeros_like(lengths)

        top = jnp.full((1, width), limit_ref[0], F32).astype(BF16)

        def clipped(ref):
            return jnp.maximum(jnp.minimum(ref[...], top), -top)

        @pl.when(step < steps)
        def _():
            all_three = dots(clipped(own_ref), matrix[...], NN) + bias_ref[...]
            q = all_three[:, :width].astype(BF16) * jnp.asarray(HD**-0.5, BF16)
            q_ref[...] = q
            kv_ref[...] = all_three[:, width:].astype(BF16)
            lengths[0:1] = jnp.maximum(lengths[0:1], head_lengths(q))

        @pl.when(step >= steps)
        def _():
            kv_ref[...] = (dots(clipped(other_ref), matrix[:, width:], NN) + bias_ref[:, width:]).astype(BF16)

        lengths[1:2] = jnp.maximum(lengths[1:2], head_lengths(kv_ref[:, :width]))

        @pl.when(step == 2 * steps - 1)
        def _():
            bound_ref[0] = jnp.max(lengths[0:1] * lengths[1:2])
            store.wait()

    any_spec = pl.BlockSpec(memory_space=pl.ANY)
    smem_spec = pl.BlockSpec(memory_space=pltpu.SMEM)
    return pl.pallas_call(
        kernel,
        grid=(2 * steps,),
        in_specs=[
            smem_spec,
            pl.BlockSpec((block, width), lambda i: (jnp.minimum(i, steps - 1), 0)),
            pl.BlockSpec((block, width), lambda i: (jnp.maximum(i - steps, 0), 0)),
            pl.BlockSpec((1, columns), lambda i: (0, 0)),
            any_spec,
            any_spec,
        ],
        out_specs=[
            pl.BlockSpec((block, width), lambda i: (jnp.minimum(i, steps - 1), 0)),
            pl.BlockSpec((block, 2 * width), lambda i: (i, 0)),
            any_spec,
            smem_spec,
        ],
        out_shape=[
            jax.ShapeDtypeStruct((rows, width), BF16),
            jax.ShapeDtypeStruct((2 * rows, 2 * width), BF16),
            jax.ShapeDtypeStruct((width, columns), BF16),
            jax.ShapeDtypeStruct((1,), F32),
        ],
        scratch_shapes=[
            pltpu.VMEM((pairs, 2, along, piece_rows, columns), BF16),
            pltpu.VMEM((8, LANES), F32),
            pltpu.SemaphoreType.DMA((2 * pairs * along + 1,)),
        ],
        compiler_params=pltpu.CompilerParams(vmem_limit_bytes=56 << 20),
        cost_estimate=SHORT,
    )(limit, tokens[0], tokens[1], biases, *pieces)


def attend(bound, queries, keys_values, start, count, filled=None):
    seqs, rows, width = queries.shape
    keys = keys_values.shape[1]
    pairs = width // LANES
    block = min(256, rows)
    held = [] if filled is None else list(filled)

    def kernel(bound_ref, q_ref, k_ref, v_ref, *refs):
        o_ref, l_ref, p_ref, token_ref = refs[len(held) :]
        low = lax.broadcasted_iota(jnp.int32, (1, LANES), 1) < HD
        token_ref[...] = jnp.zeros_like(token_ref)

        def fill(at, shifted):
            q = q_ref[0, at]
            outs, inverses = [], []
            for half in range(2):
                mine = low if half == 0 else ~low
                scores = dots(jnp.where(mine, q, jnp.zeros_like(q)), k_ref[0], NT)
                if shifted:
                    scores = scores - jnp.max(scores, axis=-1, keepdims=True)
                weights = jnp.exp(scores)
                inverse = 1.0 / jnp.sum(weights, axis=-1, keepdims=True)
                weights = weights.astype(BF16)
                p_ref[0, half, at] = weights
                outs.append(dots(weights, v_ref[0], NN) * inverse)
                inverses.append(inverse)
            o_ref[0, at] = jnp.where(low, outs[0], outs[1]).astype(BF16)
            l_ref[0, at] = jnp.where(low, inverses[0], inverses[1])

        small = bound_ref[0] < SAFE_SCORE**2

        @pl.when(small)
        def _():
            fill(slice(None), False)

        @pl.when(jnp.logical_not(small))
        def _():
            @pl.loop(0, block // 128)
            def _(number):
                fill(pl.ds(pl.multiple_of(number * 128, 128), 128), True)

    rows_spec = pl.BlockSpec((1, block, LANES), lambda s, p, i: (s, i, start + p))
    return pl.pallas_call(
        kernel,
        grid=(seqs, count, rows // block),
        in_specs=[
            pl.BlockSpec(memory_space=pltpu.SMEM),
            rows_spec,
            pl.BlockSpec((1, keys, LANES), lambda s, p, i: (s, 0, start + p)),
            pl.BlockSpec((1, keys, LANES), lambda s, p, i: (s, 0, pairs + start + p)),
        ]
        + [pl.BlockSpec(memory_space=pl.ANY)] * len(held),
        out_specs=[
            rows_spec,
            rows_spec,
            pl.BlockSpec((1, 2, block, keys), lambda s, p, i: (s, start + p, i, 0)),
            pl.BlockSpec((8, LANES), lambda s, p, i: (0, 0)),
        ],
        out_shape=[
            jax.ShapeDtypeStruct((seqs, rows, width), BF16),
            jax.ShapeDtypeStruct((seqs, rows, width), F32),
            jax.ShapeDtypeStruct((seqs, 2 * pairs, rows, keys), BF16),
            jax.ShapeDtypeStruct((8, LANES), F32),
        ],
        input_output_aliases={4 + i: i for i in range(len(held))},
        compiler_params=pltpu.CompilerParams(vmem_limit_bytes=56 << 20),
        cost_estimate=SHORT,
    )(bound, queries, keys_values, keys_values, *held)


def attend_back(queries, keys_values, context, inverse, context_grad, weights, start, count, filled=None):
    seqs, rows, width = queries.shape
    keys = keys_values.shape[1]
    pairs = width // LANES
    block = min(512, rows)
    held = [] if filled is None else list(filled)

    def kernel(q_ref, k_ref, v_ref, o_ref, l_ref, do_ref, p_ref, *refs):
        dq_ref, dk_ref, dv_ref, sums_ref, token_ref, dk_sum, dv_sum = refs[len(held) :]
        step = pl.program_id(2)
        low = lax.broadcasted_iota(jnp.int32, (1, LANES), 1) < HD
        q, do = q_ref[0], (do_ref[0].astype(F32) * l_ref[0]).astype(BF16)
        product = do.astype(F32) * o_ref[0].astype(F32)
        q_turned, do_turned = q.T, do.T

        @pl.when(step == 0)
        def _():
            dk_sum[...] = jnp.zeros_like(dk_sum)
            dv_sum[...] = jnp.zeros_like(dv_sum)
            sums_ref[...] = jnp.zeros_like(sums_ref)
            token_ref[...] = jnp.zeros_like(token_ref)

        grads = []
        for half in range(2):
            mine = low if half == 0 else ~low
            lanes = slice(half * HD, (half + 1) * HD)
            delta = jnp.sum(jnp.where(mine, product, 0.0), axis=-1, keepdims=True)
            raised = dots(jnp.where(mine, do, jnp.zeros_like(do)), v_ref[0], NT)
            p = p_ref[0, half]
            ds = (raised - delta).astype(BF16) * p
            grads.append(dots(ds, k_ref[0], NN))
            dk_sum[lanes] += dots(q_turned[lanes], ds, NN)
            dv_sum[lanes] += dots(do_turned[lanes], p, NN)
        dq = (jnp.where(low, grads[0], grads[1]) * HD**-0.5).astype(BF16)
        dq_ref[0] = dq
        sums_ref[0, 0:1] += jnp.sum(dq.astype(F32), axis=0, keepdims=True)

        @pl.when(step == pl.num_programs(2) - 1)
        def _():
            dk_ref[0] = dk_sum[...].T.astype(BF16)
            dv = dv_sum[...].T.astype(BF16)
            dv_ref[0] = dv
            sums_ref[0, 1:2] = jnp.sum(dv.astype(F32), axis=0, keepdims=True)

    rows_spec = pl.BlockSpec((1, block, LANES), lambda s, p, i: (s, i, start + p))
    keys_spec = pl.BlockSpec((1, keys, LANES), lambda s, p, i: (s, 0, start + p))
    return pl.pallas_call(
        kernel,
        grid=(seqs, count, rows // block),
        in_specs=[
            rows_spec,
            keys_spec,
            pl.BlockSpec((1, keys, LANES), lambda s, p, i: (s, 0, pairs + start + p)),
            rows_spec,
            rows_spec,
            rows_spec,
            pl.BlockSpec((1, 2, block, keys), lambda s, p, i: (s, start + p, i, 0)),
        ]
        + [pl.BlockSpec(memory_space=pl.ANY)] * len(held),
        out_specs=[
            rows_spec,
            keys_spec,
            keys_spec,
            pl.BlockSpec((1, 8, LANES), lambda s, p, i: (s, 0, start + p)),
            pl.BlockSpec((8, LANES), lambda s, p, i: (0, 0)),
        ],
        out_shape=[
            jax.ShapeDtypeStruct((seqs, rows, width), BF16),
            jax.ShapeDtypeStruct((seqs, keys, width), BF16),
            jax.ShapeDtypeStruct((seqs, keys, width), BF16),
            jax.ShapeDtypeStruct((seqs, 8, width), F32),
            jax.ShapeDtypeStruct((8, LANES), F32),
        ],
        input_output_aliases={7 + i: i for i in range(len(held))},
        scratch_shapes=[pltpu.VMEM((LANES, keys), F32), pltpu.VMEM((LANES, keys), F32)],
        compiler_params=pltpu.CompilerParams(vmem_limit_bytes=56 << 20),
        cost_estimate=SHORT,
    )(queries, keys_values, keys_values, context, inverse, context_grad, weights, *held)


def back_to_tokens(terms, matrix, first_row, rows, finish=None, pieces=1):
    width, columns = matrix.shape
    block = rows // pieces if pieces > 1 else min(512, rows)
    shift = first_row // block
    extra = [] if finish is None else list(finish)

    def kernel(*refs):
        matrix_ref, parts, refs = refs[0], refs[1 : 1 + len(terms)], refs[1 + len(terms) :]
        total = None
        for ref, (part, column) in zip(parts, terms):
            product = dots(ref[...], matrix_ref[:, column : column + part.shape[1]], NT)
            total = product if total is None else total + product
        if finish is not None:
            limit_ref, arrived_ref, zero_ref, tokens_ref, *outs = refs
            total = total + arrived_ref[...].astype(F32)
            inside = jnp.abs(tokens_ref[...].astype(F32)) < limit_ref[0]
            total = zero_ref[...].astype(F32) + jnp.where(inside, total, 0.0)
        else:
            outs = refs
        if pieces == 1:
            outs[0][...] = total.astype(BF16)
        for number, out in enumerate(outs if pieces > 1 else []):

            @pl.when(pl.program_id(0) == number)
            def _(out=out):
                out[...] = total.astype(BF16)

    row_spec = pl.BlockSpec((block, width), lambda i: (i, 0))
    return pl.pallas_call(
        kernel,
        grid=(rows // block,),
        in_specs=[pl.BlockSpec((width, columns), lambda i: (0, 0), pipeline_mode=pl.Buffered(1))]
        + [pl.BlockSpec((block, part.shape[1]), lambda i: (shift + i, 0)) for part, _ in terms]
        + ([] if finish is None else [pl.BlockSpec(memory_space=pltpu.SMEM)] + [row_spec] * 3),
        out_specs=row_spec if pieces == 1 else [pl.BlockSpec((block, width), lambda i: (0, 0))] * pieces,
        out_shape=(
            jax.ShapeDtypeStruct((rows, width), BF16)
            if pieces == 1
            else [jax.ShapeDtypeStruct((block, width), BF16)] * pieces
        ),
        compiler_params=pltpu.CompilerParams(vmem_limit_bytes=56 << 20),
        cost_estimate=SHORT,
    )(matrix, *[part for part, _ in terms], *extra)


def weight_grads(limit, tokens, chunks, sums, shape):
    rows, width = tokens[0].shape
    block = min(512, rows)
    steps = rows // block
    spans = [chunk[0].shape[1] for chunk in chunks]
    columns = 3 * width + LANES
    pairs, along = shape
    piece_rows = width // (2 * pairs * along)

    def kernel(limit_ref, own_ref, other_ref, sums_ref, *refs):
        grads, (mine_ref, theirs_ref, total, held, sems) = refs[: 3 * len(chunks)], refs[3 * len(chunks) :]
        step = pl.program_id(0)
        core = lax.axis_index("core")
        top = jnp.full((1, width), limit_ref[0], F32).astype(BF16)

        @pl.when(step == 0)
        def _():
            total[...] = jnp.zeros_like(total)

        def add(tokens_ref, kinds):
            turned = jnp.maximum(jnp.minimum(tokens_ref[...], top), -top).T
            for number, span in enumerate(spans):
                for kind in kinds:
                    start = width * kind + sum(spans[:number])
                    total[:, start : start + span] += dots(turned, grads[3 * number + kind][...], NN)

        @pl.when(step < steps)
        def _():
            add(own_ref, (0, 1, 2))

        @pl.when(step >= steps)
        def _():
            add(other_ref, (1, 2))

        @pl.when(step == 2 * steps - 1)
        def _():
            part = held.shape[:-1]
            held[..., : 3 * width] = total[...].astype(BF16).reshape(part + (3 * width,))
            rows_of = jnp.concatenate([sums_ref[...], jnp.zeros((LANES - sums_ref.shape[0], width), F32)], axis=0)
            held[..., 3 * width :] = rows_of.T.astype(BF16).reshape(part + (LANES,))
            stores = []
            for far in range(pairs):
                for number, (target, half) in enumerate(((mine_ref, core), (theirs_ref, 1 - core))):
                    stores.append(pltpu.make_async_copy(held.at[far, half], target.at[far], sems.at[2 * far + number]))
            for copy in stores:
                copy.start()
            for copy in stores:
                copy.wait()

    smem_spec = pl.BlockSpec(memory_space=pltpu.SMEM)

    def specs(span):
        own_spec = pl.BlockSpec((block, span), lambda i: (jnp.minimum(i, steps - 1), 0))
        return [own_spec] + [pl.BlockSpec((block, span), lambda i: (i, 0))] * 2

    part = jax.ShapeDtypeStruct((pairs, along, piece_rows, columns), BF16)
    return pl.pallas_call(
        kernel,
        grid=(2 * steps,),
        in_specs=[
            smem_spec,
            pl.BlockSpec((block, width), lambda i: (jnp.minimum(i, steps - 1), 0)),
            pl.BlockSpec((block, width), lambda i: (jnp.maximum(i - steps, 0), 0)),
            pl.BlockSpec(sums.shape, lambda i: (0, 0)),
        ]
        + [spec for span in spans for spec in specs(span)],
        out_specs=[pl.BlockSpec(memory_space=pl.ANY)] * 2,
        out_shape=[part, part],
        scratch_shapes=[
            pltpu.VMEM((width, 3 * width), F32),
            pltpu.VMEM((pairs, 2, along, piece_rows, columns), BF16),
            pltpu.SemaphoreType.DMA((2 * pairs,)),
        ],
        compiler_params=pltpu.CompilerParams(vmem_limit_bytes=56 << 20),
        cost_estimate=SHORT,
    )(limit, tokens[0], tokens[1], sums, *[grad for chunk in chunks for grad in chunk])


def middle(context, residual, cotangent, weights, vectors, up_bias, shape):
    rows, width = residual.shape
    units = up_bias.shape[1]
    pairs, along = shape
    block = min(256, rows)
    blocks = units // width
    parts = len(weights)
    whole = parts == 2
    share = width // (2 * pairs * along)
    if whole:
        first_shape = (pairs, 2, along * share, width + units)
        second_shape = (pairs, 2, along * share * blocks, width)
    else:
        first_shape = (pairs, 2, along, share, width + units)
        second_shape = (pairs, 2, along, blocks, share, width)
    copies = 2 if whole else 2 * pairs * (1 + blocks)

    def kernel(residual_ref, cot_ref, vector_ref, bias_ref, *refs):
        context_ref, refs = refs[0], refs[1:]
        weight_refs, refs = refs[:parts], refs[parts:]
        result_ref, zero_ref, back_ref, packed_ref, *outs, small_ref, small_up_ref, first, second, grad_output, grad_up, grad_down = refs[:-3]
        act_ref, slope_ref, sems = refs[-3:]
        step = pl.program_id(0)
        pair, core = lax.axis_index("pair"), lax.axis_index("core")

        def matches(pieces):
            if whole:
                return [(pieces[0], first), (pieces[1], second)]
            found = []
            for piece, place, half in pieces:
                found.append((piece.at[:, :, : width + units], first.at[place, half]))
                for j in range(blocks):
                    lanes = slice(width + units + width * j, width + units + width * (j + 1))
                    found.append((piece.at[:, :, lanes], second.at[place, half].at[:, j]))
            return found

        halves = core, 1 - core
        if whole:
            sources, targets = weight_refs, outs
        else:
            sources = [(ref, pair ^ (i // 2), halves[i % 2]) for i, ref in enumerate(weight_refs)]
            targets = [(out.at[far], pair ^ far, half) for far in range(pairs) for out, half in zip(outs, halves)]
        loads = [
            pltpu.make_async_copy(outside, place, sems.at[i]) for i, (outside, place) in enumerate(matches(sources))
        ]

        @pl.when(step == 0)
        def _():
            for copy in loads:
                copy.start()
            small_ref[...] = jnp.zeros_like(small_ref)
            small_up_ref[...] = jnp.zeros_like(small_up_ref)
            grad_output[...] = jnp.zeros_like(grad_output)
            grad_up[...] = jnp.zeros_like(grad_up)
            grad_down[...] = jnp.zeros_like(grad_down)
            for copy in loads:
                copy.wait()

        def vector(number):
            return vector_ref[number : number + 1]

        def mean(values):
            return jnp.mean(values, axis=-1, keepdims=True)

        def columns(j):
            return slice(width * j, width * (j + 1))

        def output_matrix():
            return first[(..., slice(0, width))].reshape(width, width)

        def up_matrix(j):
            return first[(..., slice(width * (j + 1), width * (j + 2)))].reshape(width, width)

        down_rows = second.reshape(units, width)

        bias_output, bias_down, gain_one, shift_one, gain_two, shift_two = [vector(i) for i in range(6)]
        ctx = context_ref[...]
        zero = residual_ref[...].astype(F32) + dots(ctx, output_matrix(), NN) + bias_output
        center = zero - mean(zero)
        scale_one = lax.rsqrt(mean(center * center) + NORM_EPS)
        normal_one = center * scale_one
        hidden = normal_one * gain_one + shift_one
        hidden_low = hidden.astype(BF16)
        summed = hidden + bias_down
        for j in range(blocks):
            up = dots(hidden_low, up_matrix(j), NN) + bias_ref[:, columns(j)]
            below = 0.5 + 0.5 * lax.erf(up * 0.7071067811865476)
            act = (up * below).astype(BF16)
            act_ref[:, columns(j)] = act
            slope = below + up * (0.3989422804014327 * jnp.exp(-0.5 * up * up))
            slope_ref[:, columns(j)] = slope.astype(BF16)
            summed = summed + dots(act, down_rows[columns(j)], NN)
        center = summed - mean(summed)
        scale_two = lax.rsqrt(mean(center * center) + NORM_EPS)
        normal_two = center * scale_two
        result_ref[...] = (normal_two * gain_two + shift_two).astype(result_ref.dtype)

        cot = cot_ref[...].astype(F32)
        scaled = cot * gain_two
        grad_summed = scale_two * (scaled - mean(scaled) - normal_two * mean(scaled * normal_two))
        down_low = grad_summed.astype(BF16)
        grad_hidden = grad_summed
        for j in range(blocks):
            lifted = dots(down_low, down_rows[columns(j)], NT) * slope_ref[:, columns(j)].astype(F32)
            up_low = lifted.astype(BF16)
            small_up_ref[:, columns(j)] += jnp.sum(up_low.astype(F32), axis=0, keepdims=True)
            grad_up[:, columns(j)] += dots(hidden_low, up_low, TN)
            grad_hidden = grad_hidden + dots(up_low, up_matrix(j), NT)
            grad_down[columns(j)] += dots(act_ref[:, columns(j)], down_low, TN)
        scaled = grad_hidden * gain_one
        grad_zero = scale_one * (scaled - mean(scaled) - normal_one * mean(scaled * normal_one))
        branch_low = grad_zero.astype(BF16)
        zero_ref[...] = branch_low
        grad_output[...] += dots(ctx, branch_low, TN)
        back_ref[...] = dots(branch_low, output_matrix(), NT).astype(BF16)
        sums = [branch_low.astype(F32), down_low.astype(F32), grad_hidden * normal_one, grad_hidden, cot * normal_two, cot]
        for number, terms in enumerate(sums):
            small_ref[number : number + 1] += jnp.sum(terms, axis=0, keepdims=True)

        @pl.when(step == pl.num_programs(0) - 1)
        def _():
            stores = [
                pltpu.make_async_copy(place, outside, sems.at[i]) for i, (outside, place) in enumerate(matches(targets))
            ]
            span = 2 if whole else 1 + blocks
            ahead = [copy for i, copy in enumerate(stores) if i % span]
            second[...] = grad_down[...].astype(BF16).reshape(second.shape)
            for copy in ahead:
                copy.start()
            part = first.shape[:-1] + (width,)
            first[(..., slice(0, width))] = grad_output[...].astype(BF16).reshape(part)
            for j in range(blocks):
                lanes = slice(width * (j + 1), width * (j + 2))
                first[(..., lanes)] = grad_up[:, columns(j)].astype(BF16).reshape(part)
            for copy in stores[::span]:
                copy.start()
            packed_ref[...] = jnp.zeros_like(packed_ref)
            for device in range(2 * pairs * along):
                packed_ref[device, :8, :share] = small_ref[:, share * device : share * (device + 1)]
                up_lanes = slice(share * blocks * device, share * blocks * (device + 1))
                packed_ref[device, 8:9, : share * blocks] = small_up_ref[:, up_lanes]
            for copy in stores:
                copy.wait()

    any_spec = pl.BlockSpec(memory_space=pl.ANY)
    row_spec = pl.BlockSpec((block, width), lambda i: (i, 0))
    if whole:
        grads = [jax.ShapeDtypeStruct(first_shape, BF16), jax.ShapeDtypeStruct(second_shape, BF16)]
    else:
        grads = [jax.ShapeDtypeStruct((pairs, along, share, width + 2 * units), BF16)] * 2
    return pl.pallas_call(
        kernel,
        grid=(rows // block,),
        in_specs=[row_spec] * 2
        + [pl.BlockSpec((8, width), lambda i: (0, 0)), pl.BlockSpec((1, units), lambda i: (0, 0))]
        + [row_spec]
        + [any_spec] * parts,
        out_specs=[row_spec] * 3
        + [pl.BlockSpec((2 * pairs * along, 16, LANES), lambda i: (0, 0, 0))]
        + [any_spec] * 2,
        out_shape=[
            jax.ShapeDtypeStruct((rows, width), BF16),
            jax.ShapeDtypeStruct((rows, width), BF16),
            jax.ShapeDtypeStruct((rows, width), BF16),
            jax.ShapeDtypeStruct((2 * pairs * along, 16, LANES), F32),
            *grads,
        ],
        scratch_shapes=[
            pltpu.VMEM((8, width), F32),
            pltpu.VMEM((1, units), F32),
            pltpu.VMEM(first_shape, BF16),
            pltpu.VMEM(second_shape, BF16),
            pltpu.VMEM((width, width), F32),
            pltpu.VMEM((width, units), F32),
            pltpu.VMEM((units, width), F32),
            pltpu.VMEM((block, units), BF16),
            pltpu.VMEM((block, units), BF16),
            pltpu.SemaphoreType.DMA((copies,)),
        ],
        compiler_params=pltpu.CompilerParams(vmem_limit_bytes=62 << 20),
        cost_estimate=SHORT,
    )(residual, cotangent, vectors, up_bias, context, *weights)


def after(values, *earlier):
    return lax.optimization_barrier((values, earlier))[0]


class Plan:
    def __init__(self, pairs, along, seqs):
        self.pairs, self.along, self.seqs = pairs, along, seqs
        self.devices = 2 * pairs * along
        self.by_chip = 2 * seqs == along and pairs == 4 and along & (along - 1) == 0

    def moves(self, number):
        table = []
        for pair in range(self.pairs):
            for core in range(2):
                for place in range(self.along):
                    source = (pair * 2 + core) * self.along + place
                    chip = core * self.seqs + (place + number) % self.seqs
                    target = (pair * 2 + 1 - place // self.seqs) * self.along + chip
                    table.append((source, target))
        return table

    def send(self, part, number, *earlier):
        return lax.ppermute(after(part, *earlier), AXES, self.moves(number))

    def send_home(self, worked):
        blocks = worked if isinstance(worked, (list, tuple)) else worked.reshape(self.seqs, -1, worked.shape[-1])
        if not self.by_chip:
            return blocks
        return [
            lax.ppermute(blocks[number], AXES, [(b, a) for a, b in self.moves(number)]) for number in range(self.seqs)
        ]

    def at_home(self, back):
        return unpack(back) if self.by_chip else back.astype(F32)

    def swap(self, values):
        return lax.ppermute(values, "core", [(0, 1), (1, 0)])

    def meet(self, values, axis, far):
        count = lax.axis_size(axis)
        return lax.ppermute(values, axis, [(i, i ^ far) for i in range(count)])

    def column(self, rows, *earlier):
        return [rows] + after([self.meet(rows, "seq", far) for far in range(1, self.along)], *earlier)

    def ordered(self, column, here):
        held = jnp.zeros((self.along,) + column[0].shape, column[0].dtype)
        for far in range(self.along):
            held = lax.dynamic_update_index_in_dim(held, column[far], here ^ far, 0)
        return held

    def both_cores(self, pieces):
        return [part for piece in pieces for part in (piece, self.swap(piece))]

    def add_cores(self, mine, theirs, *earlier):
        theirs = after(self.swap(theirs), *earlier)
        return (mine.astype(F32) + theirs.astype(F32)).astype(BF16)

    def add_blocks(self, mine, theirs, *earlier):
        theirs = after(self.swap(theirs), *earlier)
        return [(mine[far].astype(F32) + theirs[far].astype(F32)).astype(BF16) for far in range(self.pairs)]

    def spread(self, column):
        copies = jnp.broadcast_to(column[None], (self.pairs,) + column.shape)
        return lax.all_to_all(copies, "pair", split_axis=0, concat_axis=0, tiled=True)

    def near_and_far(self, column):
        return [column] + [self.meet(column, "pair", far) for far in range(1, self.pairs)]

    def total_along(self, values, *earlier):
        return self.gathered(values, "seq", *earlier)

    def gathered(self, parts, axis, *earlier):
        arrived = after([self.meet(parts[far], axis, far) for far in range(1, len(parts))], *earlier)
        total = parts[0].astype(F32)
        for part in arrived:
            total = total + part.astype(F32)
        return total

    def total(self, parts, axis):
        arrived = lax.all_to_all(parts, axis, split_axis=0, concat_axis=0, tiled=True)
        return jnp.sum(arrived.astype(F32), axis=0)

    def everywhere(self, values):
        copies = jnp.broadcast_to(values[None], (self.devices,) + values.shape)
        return lax.all_to_all(copies, AXES, split_axis=0, concat_axis=0, tiled=True)

    def exchange(self, parts):
        return lax.all_to_all(parts, AXES, split_axis=0, concat_axis=0, tiled=True)

    def gather(self, rows):
        return lax.all_gather(rows, AXES, axis=0, tiled=True)

    def scatter(self, total):
        return lax.psum_scatter(total, AXES, scatter_dimension=0, tiled=True)


def local(plan, tokens, cotangent, *rest):
    params, clip_limits = rest[:15], rest[15]
    limit = clip_limits[0]
    matrices = params[:6]
    width = tokens.shape[-1]
    units = matrices[4].shape[1]
    devices = plan.devices

    chosen, place = parcel(tokens, clip_limits)
    if plan.by_chip:
        qkv_rows, rest_rows, packed = prepare(matrices, params[6:])
        qkv_column = jnp.stack(plan.column(qkv_rows))
        vectors = plan.everywhere(packed)
        coarse = jnp.concatenate([plan.send(part, i) for i, part in enumerate(chosen)], axis=0)
        vectors = vectors.astype(F32)
        sizes = [vector.shape[0] for vector in params[6:]]
        vectors, terms = [vectors[:, i, :size].reshape(-1) for i, size in enumerate(sizes)], vectors[:, len(sizes), :18]
        limits = 0.5 * jnp.max(terms[:, :6] + terms[:, 6:12] + terms[:, 12:18], axis=0)
    else:
        coarse = jnp.roll(jnp.stack(chosen), place, axis=0).reshape(-1, width)
        vectors = [lax.all_gather(vector.astype(BF16), AXES, axis=0, tiled=True).astype(F32) for vector in params[6:]]
        limits = 0.5 * lax.pmax(jnp.stack([jnp.max(jnp.abs(matrix)) for matrix in matrices]), AXES)
    bias_query, bias_value, bias_output, bias_up, bias_down, gain_one, shift_one, gain_two, shift_two = vectors
    biases = jnp.concatenate([bias_query, jnp.zeros_like(bias_value), bias_value])[None]
    limit_low = limit.astype(BF16)

    def clip_to(number):
        return jnp.clip(matrices[number], -limits[number], limits[number]).astype(BF16)

    if plan.by_chip:
        seqs, keys = 1, 2 * coarse.shape[0]
        chosen_cotangent = parcel(after(cotangent, chosen), None)[0]
        ceilings = [jnp.full((size,), top, BF16) for size, top in zip((width, units, units), limits[3:].astype(BF16))]
        ceilings = jnp.concatenate(ceilings)[None, None]
        rest_column = plan.ordered(plan.column(after(rest_rows, qkv_column)), place)
        rest_column = jnp.clip(rest_column, -ceilings, ceilings)
        rest_pieces = plan.near_and_far(rest_column)
        qkv_same = plan.spread(qkv_column)
        qkv_across = plan.swap(qkv_same)
        coarse, chosen_cotangent = after((coarse, chosen_cotangent), rest_column, qkv_across)
        other = plan.swap(coarse)
        queries, keys_values, matrix, bound = project(clip_limits, [coarse, other], [qkv_same, qkv_across], biases)
        cotangent_low = [plan.send(chosen_cotangent[0], 0)]
        cotangent_low += [plan.send(part, i + 1, queries) for i, part in enumerate(chosen_cotangent[1:])]
    else:
        seqs = tokens.shape[0]
        every = lax.all_gather(coarse.reshape(tokens.shape), "seq", axis=1, tiled=True)
        keys = every.shape[1]
        every = every.reshape(-1, width)
        matrix = plan.gather(jnp.concatenate([matrix.astype(BF16) for matrix in matrices[:3]], axis=1))
        ceilings = jnp.repeat(limits[:3].astype(BF16), width)[None]
        matrix = jnp.clip(matrix, -ceilings, ceilings)
        all_keys = jnp.clip(every, -limit_low, limit_low)
        clipped = jnp.clip(coarse, -limit_low, limit_low)
        queries = dots(clipped, matrix[:, :width], NN) + biases[:, :width]
        queries = queries.astype(BF16) * jnp.asarray(HD**-0.5, BF16)
        keys_values = (dots(all_keys, matrix[:, width:], NN) + biases[:, width:]).astype(BF16)
        lengths = [
            jnp.sum(jnp.square(part.astype(F32)).reshape(-1, width // HD, HD), axis=-1).max(axis=0)
            for part in (queries, keys_values[:, :width])
        ]
        bound = jnp.max(lengths[0] * lengths[1])[None]
        cotangent_low = cotangent.astype(BF16).reshape(-1, width)
        rest_weights = [
            plan.gather(jnp.concatenate([clip_to(3), clip_to(4)], axis=1)).reshape(plan.pairs, 2, -1, width + units),
            plan.gather(clip_to(5)).reshape(plan.pairs, 2, -1, width),
        ]
    rows = coarse.shape[0] // seqs

    queries = queries.reshape(seqs, rows, width)
    keys_values = keys_values.reshape(seqs, keys, 2 * width)
    filled = None
    for number, count in enumerate(GROUPS):
        *filled, token = attend(bound, queries, keys_values, sum(GROUPS[:number]), count, filled)
        queries, keys_values = after((queries, keys_values), token)
    if plan.by_chip:
        cotangent_low = jnp.concatenate(cotangent_low, axis=0)
        rest_pieces = after(rest_pieces, token, cotangent_low)
        rest_weights = plan.both_cores(rest_pieces)
    context, inverse, weights = filled
    six = [bias_output, bias_down, gain_one, shift_one, gain_two, shift_two]
    six = jnp.stack(six + [jnp.zeros_like(bias_down)] * 2)
    result, grad_zero, context_grad, small, *grads = middle(
        context.reshape(-1, width),
        coarse,
        cotangent_low,
        rest_weights,
        six,
        bias_up[None],
        (plan.pairs, plan.along),
    )
    layer_out = result if plan.by_chip else plan.send_home(result)
    mids = grads
    small = plan.exchange(small)

    context_grad = context_grad.reshape(seqs, rows, width)
    filled = None
    for number, count in enumerate(BACK_GROUPS):
        *filled, token = attend_back(
            queries, keys_values, context, inverse, context_grad, weights, sum(BACK_GROUPS[:number]), count, filled
        )
        if plan.by_chip and number == 0:
            low = plan.add_blocks(mids[0], mids[1], token)
            context_grad, low = after((context_grad, low))
            rest_sum = plan.gathered(low, "pair").astype(BF16)
            layer_out = plan.send_home(after(result, token))
        context_grad = after(context_grad, token)
    grads = [grad.reshape(-1, width) for grad in filled[:3]]
    sums = jnp.sum(filled[3], axis=0)
    key_terms = [(grads[1], width), (grads[2], 2 * width)]
    local_rows = coarse.shape[0]
    if plan.by_chip:
        leaving = back_to_tokens(key_terms, matrix, local_rows, local_rows)
        arrived = plan.swap(leaving)
        layer_out, rest_sum, small, grads = after((layer_out, rest_sum, small, grads), leaving)
        rest_sum = [
            lax.dynamic_index_in_dim(rest_sum, place ^ far, 0, keepdims=False) for far in range(plan.along)
        ]
        rest_sum, sums = after((rest_sum, sums))
        mine, theirs = weight_grads(clip_limits, [coarse, other], [grads], sums, (plan.pairs, plan.along))
        late = plan.add_cores(mine, theirs)
        arrived, late = after((arrived, late))
        own_terms = [(grads[0], 0)] + key_terms
    else:
        partial = back_to_tokens(key_terms, matrix, 0, seqs * keys).reshape(seqs, keys, width)
        arrived = lax.psum_scatter(partial, "seq", scatter_dimension=1, tiled=True).reshape(-1, width)
        own_terms = [(grads[0], 0)]
    tokens_grad = back_to_tokens(
        own_terms, matrix, 0, local_rows, (clip_limits, arrived, grad_zero, coarse), plan.seqs if plan.by_chip else 1
    )
    if plan.by_chip:
        rest_parts = after([plan.meet(rest_sum[far], "seq", far) for far in range(1, plan.along)], tokens_grad)
        tokens_grad, rest_parts = after((tokens_grad, rest_parts))
        late = plan.total(late, "pair").astype(BF16)
        rest_grad = rest_sum[0].astype(F32)
        for part in rest_parts:
            rest_grad = rest_grad + part.astype(F32)
        late = plan.total(late, "seq")
        layer_out = after(layer_out, tokens_grad)
        bias_grads = [late[:, 3 * width + i] for i in range(2)]
        first_grad, second_grad = rest_grad[:, : width + units], rest_grad[:, width + units :]
        second_grad = jnp.concatenate(jnp.split(second_grad, units // width, axis=1), axis=0)
    else:
        late = [
            dots(left, grads[kind], TN) for kind, left in enumerate((clipped, all_keys, all_keys))
        ]
        late = plan.scatter(jnp.concatenate(late, axis=1))
        bias_grads = [plan.scatter(sums[i]) for i in range(2)]
        first_grad = plan.scatter(mids[0].reshape(width, -1)).astype(F32)
        second_grad = plan.scatter(mids[1].reshape(units, -1)).astype(F32)
    tokens_grad = plan.at_home(plan.send_home(tokens_grad))
    small = jnp.sum(after(small, tokens_grad), axis=0)
    small_up = small[8, : units // devices]
    share = width // devices
    small = [small[i, :share] for i in range(6)]
    small = [*bias_grads, small[0], small_up, *small[1:]]

    shares = [late[:, :width], late[:, width : 2 * width], late[:, 2 * width : 3 * width]]
    shares += [first_grad[:, :width], first_grad[:, width:], second_grad]
    masked = [
        jnp.where(jnp.abs(matrices[number]) < limits[number], shares[number], 0.0) for number in range(6)
    ]
    return (
        plan.at_home(layer_out),
        tokens_grad,
        *masked,
        *small,
    )


def solution(mesh):
    pairs, along = mesh.shape["batch"] // 2, mesh.shape["seq"]
    fine_mesh = Mesh(mesh.devices.reshape(pairs, 2, along), AXES)
    rows = P(("pair", "core"), "seq", None)
    matrix = P(AXES, None)
    vector = P(AXES)

    def whole(tokens, *rest):
        plan = Plan(pairs, along, tokens.shape[0] // (2 * pairs))

        def run(*args):
            return local(plan, *args)

        return jax.shard_map(
            run,
            mesh=fine_mesh,
            in_specs=(rows, rows) + (matrix,) * 6 + (vector,) * 9 + (P(),),
            out_specs=(rows, rows) + (matrix,) * 6 + (vector,) * 9,
            check_vma=False,
        )(tokens, *rest)

    return whole
```
